128 devices in a mesh: gz: 128 (over z, y, x, core).
Axes of the slice: x: 4, y: 4, z: 4, core: 2. Of those that a mesh axis runs over, the one named last changes fastest.
Arguments:
- order_param: float32 [128, 512, 512], P('gz'), may hold values from 0.05 to 0.95
- concentration: float32 [128, 512, 512], P('gz'), may hold values from 0 to 1
- strain: float32 [6, 128, 512, 512], P(None, 'gz'), may hold values from -6 to 6
- grain_ids: int32 [128, 512, 512], P('gz'), may hold values from 0 to 15
- seed_labels: int32 [128, 512, 512], P('gz'), may hold values from 0 to 8
- grain_moduli: float32 [2, 16], replicated, may hold values from 0.5 to 2
- grain_mobility: float32 [16], replicated, may hold values from 0.25 to 1
- seed_rate: float32 [8], replicated, may hold values from 0.5 to 4
Outputs:
- order_next: float32 [128, 512, 512], P('gz')
- conc_next: float32 [128, 512, 512], P('gz')
- strain_next: float32 [6, 128, 512, 512], P(None, 'gz')
The draws below stay inside these ranges and needn't reach their ends.
Inputs may be any that keep to these rules, and one draw needn't show every extreme that they name: `seed_labels`: 0 marks a voxel without seed; label k > 0 names entry k - 1 of seed_rate.
All inputs are finite; a program needn't handle non-finite values.
Results may differ from the reference program's by a relative error of at most 0.0003.
Values sent between devices are 32-bit elements; how exact they have to be, the bound alone decides.
No kernel may reach another device: no remote copies, remote signals or barrier semaphores. Data moves between devices by JAX's collectives and lax.ppermute only.
A program may use at most 256 MiB of HBM per device.

```python
import math
import jax
import jax.numpy as jnp
from jax import lax

NX = 512
NY = 512
GRAINS = 16
SEEDS = 8
SUBSTEPS = 2
NZ = 128


def touch_ends(values, own_key, least, largest):
    longest = values.shape.index(max(values.shape))
    spots = []
    for shift in (0, 1):
        where = [jax.random.randint(jax.random.fold_in(own_key, axis), (), 0, length) for axis, length in enumerate(values.shape)]
        where[longest] = (where[longest] + shift) % values.shape[longest]
        spots.append(tuple(where))
    return values.at[spots[0]].set(least).at[spots[1]].set(largest)


def shard_levels(rng, shape, pieces, least, largest):
    def one(dim, blocks):
        heights = jax.random.uniform(jax.random.fold_in(jax.random.fold_in(rng, 6), dim), (blocks,), jnp.float32, least / len(pieces), largest / len(pieces))
        return jnp.repeat(jnp.exp(heights), shape[dim] // blocks).reshape((-1,) + (1,) * (len(shape) - dim - 1))

    loudness = one(*pieces[0])
    for cut in pieces[1:]:
        loudness = loudness * one(*cut)
    return loudness


def noise(rng, shape, spread, bound, split=(), kind=jnp.bfloat16):
    array = spread * jax.random.normal(rng, shape, jnp.float32)
    if split:
        array = array * shard_levels(rng, shape, split, -0.22, 0.18)
    return jnp.clip(array, -bound, bound).astype(kind)


def setup_inputs(seed: int = 0) -> dict:
    splits = jax.random.split(jax.random.key(seed), 9)
    order_param = jnp.clip(0.05 + 0.9 * jax.random.uniform(splits[0], (NZ, NY, NX), jnp.float32) ** shard_levels(splits[0], (NZ, NY, NX), ((0, 128),), -0.2, 0.2), 0.05, 0.95)
    concentration = jnp.clip(1.0 * jax.random.uniform(splits[1], (NZ, NY, NX), jnp.float32) ** shard_levels(splits[1], (NZ, NY, NX), ((0, 128),), -0.2, 0.2), 0.0, 1.0)
    strain = noise(splits[2], (6, NZ, NY, NX), 1.0, 6.0, ((1, 128),), jnp.float32)
    grain_ids = touch_ends(jax.random.randint(splits[3], (NZ, NY, NX), 0, GRAINS), jax.random.fold_in(splits[3], 1), 0, GRAINS - 1).astype(jnp.int32)
    seed_labels = touch_ends(jax.random.randint(splits[4], (NZ, NY, NX), 0, SEEDS + 1), jax.random.fold_in(splits[4], 1), 0, SEEDS).astype(jnp.int32)
    grain_moduli = jnp.clip(jnp.exp(jax.random.uniform(splits[5], (2, GRAINS), jnp.float32, math.log(0.5), math.log(2.0))), 0.5, 2.0)
    grain_mobility = jnp.clip(jnp.exp(jax.random.uniform(splits[6], (GRAINS,), jnp.float32, math.log(0.25), math.log(1.0))), 0.25, 1.0)
    seed_rate = jnp.clip(jnp.exp(jax.random.uniform(splits[7], (SEEDS,), jnp.float32, math.log(0.5), math.log(4.0))), 0.5, 4.0)
    return {"order_param": order_param, "concentration": concentration, "strain": strain, "grain_ids": grain_ids, "seed_labels": seed_labels, "grain_moduli": grain_moduli, "grain_mobility": grain_mobility, "seed_rate": seed_rate}


time_step = 0.05
grad_coef = 1.0
well_height = 1.0
drive_coef = 2.0
conc_eq = 0.5
mech_boost = 1.0
diffusivity = 1.0
release_coef = 1.0
residual_stiff = 0.1
lame_ref = 1.0
shear_ref = 1.0
coupling = (lame_ref + shear_ref) / (shear_ref * (lame_ref + 2.0 * shear_ref))


def laplace(field):
    z_sum = jnp.roll(field, 1, 0) + jnp.roll(field, -1, 0)
    y_sum = jnp.roll(field, 1, 1) + jnp.roll(field, -1, 1)
    x_sum = jnp.roll(field, 1, 2) + jnp.roll(field, -1, 2)
    return z_sum + y_sum + x_sum - 6.0 * field


def advance(order_now, conc_now, lap_order, lap_conc, kinetic, decay):
    well_grad = 2.0 * order_now * (1.0 - order_now) * (1.0 - 2.0 * order_now)
    interp_grad = 6.0 * order_now * (1.0 - order_now)
    force = grad_coef * lap_order - well_height * well_grad + drive_coef * interp_grad * (conc_now - conc_eq)
    order_new = order_now + kinetic * force - decay * order_now
    conc_new = conc_now + time_step * diffusivity * lap_conc + release_coef * (order_now - order_new)
    return order_new, conc_new


def coefficients(strain, lame, shear, mobility, rate):
    trace = strain[0] + strain[1] + strain[2]
    square = strain[0] * strain[0] + strain[1] * strain[1] + strain[2] * strain[2] + 2.0 * (strain[3] * strain[3] + strain[4] * strain[4] + strain[5] * strain[5])
    energy = 0.5 * lame * trace * trace + shear * square
    mech = 1.0 + mech_boost * energy / (1.0 + energy)
    kinetic = time_step * mobility * mech
    decay = time_step * rate
    return kinetic, decay


def stress_of(strain, order_now, lame, shear):
    scale = order_now * order_now * (3.0 - 2.0 * order_now) + residual_stiff
    lame_now = scale * lame
    shear_now = scale * shear
    trace = strain[0] + strain[1] + strain[2]
    parts = []
    for comp in range(6):
        if comp < 3:
            parts.append(lame_now * trace + 2.0 * shear_now * strain[comp])
        else:
            parts.append(2.0 * shear_now * strain[comp])
    return jnp.stack(parts)


def green(tau, xi_x, xi_y, xi_z, limit):
    t_xx, t_yy, t_zz, t_yz, t_xz, t_xy = tau
    v_x = t_xx * xi_x + t_xy * xi_y + t_xz * xi_z
    v_y = t_xy * xi_x + t_yy * xi_y + t_yz * xi_z
    v_z = t_xz * xi_x + t_yz * xi_y + t_zz * xi_z
    inner = xi_x * v_x + xi_y * v_y + xi_z * v_z
    wave_sq = xi_x * xi_x + xi_y * xi_y + xi_z * xi_z
    live = (wave_sq > 0.5) & (xi_x < limit)
    safe_sq = jnp.where(live, wave_sq, 1.0)
    first = jnp.where(live, 1.0 / (2.0 * shear_ref * safe_sq), 0.0)
    second = jnp.where(live, coupling / (safe_sq * safe_sq), 0.0)
    xis = (xi_x, xi_y, xi_z)
    vees = (v_x, v_y, v_z)
    pairs = ((0, 0), (1, 1), (2, 2), (1, 2), (0, 2), (0, 1))
    result = []
    for left, right in pairs:
        term = (xis[right] * vees[left] + xis[left] * vees[right]) * first - xis[left] * xis[right] * inner * second
        result.append(term)
    return result


def signed_waves(count):
    index = jnp.arange(count, dtype=jnp.int32)
    return jnp.where(index < count // 2, index, index - count).astype(jnp.float32)


def reference(order_param, concentration, strain, grain_ids, seed_labels, grain_moduli, grain_mobility, seed_rate):
    lame = grain_moduli[0][grain_ids]
    shear = grain_moduli[1][grain_ids]
    mobility = grain_mobility[grain_ids]
    seed_index = jnp.maximum(seed_labels - 1, 0).astype(jnp.int32)
    rate = jnp.where(seed_labels > 0, seed_rate[seed_index], jnp.zeros_like(seed_rate[seed_index]))
    kinetic, decay = coefficients(strain, lame, shear, mobility, rate)
    order_now = order_param
    conc_now = concentration
    for step_index in range(SUBSTEPS):
        order_now, conc_now = advance(order_now, conc_now, laplace(order_now), laplace(conc_now), kinetic, decay)
    stress = stress_of(strain, order_now, lame, shear)
    spectrum = jnp.fft.rfftn(stress, axes=(1, 2, 3))
    xi_z = signed_waves(NZ)
    xi_y = signed_waves(NY)[:, None]
    xi_x = jnp.arange(NX // 2 + 1).astype(jnp.float32)
    limit = float(NX // 2)

    def plane(item):
        tau_plane, wave_z = item
        return jnp.stack(green([tau_plane[comp] for comp in range(6)], xi_x, xi_y, wave_z, limit))

    planes = lax.map(plane, (jnp.moveaxis(spectrum, 1, 0), xi_z))
    increment = jnp.fft.irfftn(jnp.moveaxis(planes, 0, 1), s=(NZ, NY, NX), axes=(1, 2, 3))
    strain_next = strain - increment
    return order_now, conc_now, strain_next
```

```python
import functools
import math

import jax
import jax.numpy as jnp
from jax import lax
from jax.experimental import pallas as pl
from jax.experimental.pallas import tpu as pltpu
from jax.sharding import PartitionSpec as P

SUBSTEPS = 2
N = 512
HALF = 256
LANE = 128
DEPTH = 128
COMPS = 6
RADIX = 4
ROWS = COMPS * RADIX * 2
BLOCK = LANE * ROWS

time_step = 0.05
grad_coef = 1.0
well_height = 1.0
drive_coef = 2.0
conc_eq = 0.5
mech_boost = 1.0
diffusivity = 1.0
release_coef = 1.0
residual_stiff = 0.1
lame_ref = 1.0
shear_ref = 1.0
coupling = (lame_ref + shear_ref) / (shear_ref * (lame_ref + 2.0 * shear_ref))

f32 = jnp.float32
bf16 = jnp.bfloat16
VMEM_LIMIT = 40 * 1024 * 1024


def params(dims=1):
    return pltpu.CompilerParams(
        dimension_semantics=("arbitrary",) * dims, vmem_limit_bytes=VMEM_LIMIT
    )


def split(value):
    high = value.astype(bf16)
    low = (value - high.astype(f32)).astype(bf16)
    return high, low


def mul(left, right):
    return lax.dot_general(
        left, right, (((1,), (0,)), ((), ())), preferred_element_type=f32
    )


def table_times(table, value):
    high, low = split(value)
    return mul(table[0], high) + mul(table[0], low) + mul(table[1], high)


def times_table(value, table):
    high, low = split(value)
    return mul(high, table[0]) + mul(low, table[0]) + mul(high, table[1])


def unit_cos(index):
    wrapped = ((index + 256) & 511) - 256
    angle = (128 - jnp.abs(wrapped)).astype(f32) * (2.0 * math.pi / 512.0)
    square = angle * angle
    poly = 1.0 / 6227020800.0
    for power in (39916800.0, 362880.0, 5040.0, 120.0, 6.0):
        poly = 1.0 / power - square * poly
    return angle * (1.0 - square * poly)


def table_body(txf_ref, mq_ref, mz_ref, mqi_ref, txi_ref):
    rows = lax.broadcasted_iota(jnp.int32, (HALF, HALF), 0)
    cols = lax.broadcasted_iota(jnp.int32, (HALF, HALF), 1)
    row_low = rows & 127
    row_top = rows >> 7
    col_low = cols & 127
    col_top = cols >> 7

    def put(ref, slot, value):
        high, low = split(value)
        ref[slot, 0] = high
        ref[slot, 1] = low

    turn = (row_top - col_top) * 128
    for parity in range(2):
        wave = 2 * col_low + parity
        put(txf_ref, parity, unit_cos(rows * wave + col_top * 128))
        wave = 2 * row_low + parity
        weight = jnp.where(wave == 0, 1.0, 2.0) * (1.0 / float(N * N * DEPTH))
        put(txi_ref, parity, unit_cos(wave * cols + row_top * 128) * weight)
    for rest in range(RADIX):
        put(mq_ref, rest, unit_cos((4 * row_low + rest) * col_low + turn))
        put(mqi_ref, rest, unit_cos((4 * col_low + rest) * row_low - turn))
    put(mz_ref, 0, unit_cos(4 * row_low * col_low + turn))
    put(mz_ref, 1, unit_cos(4 * row_low * col_low - turn))


def make_tables():
    shape = lambda count: jax.ShapeDtypeStruct((count, 2, HALF, HALF), bf16)
    return pl.pallas_call(
        table_body,
        out_shape=(shape(2), shape(4), shape(2), shape(4), shape(2)),
        compiler_params=pltpu.CompilerParams(vmem_limit_bytes=VMEM_LIMIT),
        name="tables",
    )()


TILE = 128
STRIP = 16


def coef_body(moduli, mobility, rates, grain_ref, label_ref, strain_ref, lame_ref_, shear_ref_, kin_ref, dec_ref):
    def strip(step, carry):
        where = pl.ds(pl.multiple_of(step * STRIP, STRIP), STRIP)
        grain = grain_ref[where, :]
        label = label_ref[where, :]
        lame = jnp.zeros(grain.shape, f32)
        shear = jnp.zeros(grain.shape, f32)
        mob = jnp.zeros(grain.shape, f32)
        rate = jnp.zeros(grain.shape, f32)
        for index in range(mobility.shape[0]):
            hit = grain == index
            lame = jnp.where(hit, moduli[0, index], lame)
            shear = jnp.where(hit, moduli[1, index], shear)
            mob = jnp.where(hit, mobility[index], mob)
        for index in range(rates.shape[0]):
            rate = jnp.where(label == index + 1, rates[index], rate)
        parts = [strain_ref[comp, where, :] for comp in range(COMPS)]
        trace = parts[0] + parts[1] + parts[2]
        square = (
            parts[0] * parts[0]
            + parts[1] * parts[1]
            + parts[2] * parts[2]
            + 2.0 * (parts[3] * parts[3] + parts[4] * parts[4] + parts[5] * parts[5])
        )
        energy = 0.5 * lame * trace * trace + shear * square
        mech = 1.0 + mech_boost * energy / (1.0 + energy)
        lame_ref_[where, :] = lame
        shear_ref_[where, :] = shear
        kin_ref[where, :] = time_step * mob * mech
        dec_ref[where, :] = time_step * rate
        return carry

    lax.fori_loop(0, TILE // STRIP, strip, 0)


def coefficients(moduli, mobility, rates, grain, label, strain):
    plane = jax.ShapeDtypeStruct((N, N), f32)
    block = pl.BlockSpec((TILE, N), lambda i: (i, 0))
    smem = pl.BlockSpec(memory_space=pltpu.SMEM)
    return pl.pallas_call(
        coef_body,
        grid=(N // TILE,),
        in_specs=[smem, smem, smem, block, block, pl.BlockSpec((COMPS, TILE, N), lambda i: (0, i, 0))],
        out_specs=[block] * 4,
        out_shape=[plane] * 4,
        compiler_params=params(),
        name="coefficients",
    )(moduli, mobility, rates, grain, label, strain)


def planar_sum(ref, start):
    center = ref[pl.ds(start, STRIP), :]
    before = ref[pl.ds(pl.multiple_of((start + N - 8) & (N - 1), 8), 8), :]
    after = ref[pl.ds(pl.multiple_of((start + STRIP) & (N - 1), 8), 8), :]
    tall = jnp.concatenate([before, center, after], axis=0)
    height = STRIP + 16
    above = pltpu.roll(tall, 1, 0)[8 : 8 + STRIP]
    below = pltpu.roll(tall, height - 1, 0)[8 : 8 + STRIP]
    sides = pltpu.roll(center, 1, 1) + pltpu.roll(center, N - 1, 1)
    return center, (above + below) + sides


def step_body(p_ref, c_ref, pu_ref, pd_ref, cu_ref, cd_ref, kin_ref, dec_ref, p_out, c_out):
    base = pl.program_id(0) * TILE

    def strip(step, carry):
        local = pl.multiple_of(step * STRIP, STRIP)
        where = pl.ds(local, STRIP)
        start = pl.multiple_of(base + local, STRIP)
        order_now, order_sum = planar_sum(p_ref, start)
        conc_now, conc_sum = planar_sum(c_ref, start)
        lap_order = order_sum + (pu_ref[where, :] + pd_ref[where, :]) - 6.0 * order_now
        lap_conc = conc_sum + (cu_ref[where, :] + cd_ref[where, :]) - 6.0 * conc_now
        slope = order_now * (1.0 - order_now)
        well_grad = 2.0 * slope * (1.0 - 2.0 * order_now)
        force = (
            grad_coef * lap_order
            - well_height * well_grad
            + drive_coef * 6.0 * slope * (conc_now - conc_eq)
        )
        order_new = order_now + kin_ref[where, :] * force - dec_ref[where, :] * order_now
        p_out[where, :] = order_new
        c_out[where, :] = (
            conc_now + time_step * diffusivity * lap_conc + release_coef * (order_now - order_new)
        )
        return carry

    lax.fori_loop(0, TILE // STRIP, strip, 0)


def substep(order_now, conc_now, halos, kinetic, decay):
    plane = jax.ShapeDtypeStruct((N, N), f32)
    whole = pl.BlockSpec((N, N), lambda i: (0, 0))
    block = pl.BlockSpec((TILE, N), lambda i: (i, 0))
    return pl.pallas_call(
        step_body,
        grid=(N // TILE,),
        in_specs=[whole, whole] + [block] * 6,
        out_specs=[block] * 2,
        out_shape=[plane] * 2,
        compiler_params=params(),
        name="substep",
    )(order_now, conc_now, *halos, kinetic, decay)


def forward_y(scratch, mq_ref, out_ref, pair):
    first = pair * 2
    mixed = []
    for comp in (0, 1):
        blocks_r = [scratch[first + comp, pl.ds(128 * j, 128), pl.ds(0, 128)] for j in range(4)]
        blocks_i = [scratch[first + comp, pl.ds(128 * j, 128), pl.ds(128, 128)] for j in range(4)]
        er0, er1 = blocks_r[0] + blocks_r[2], blocks_r[0] - blocks_r[2]
        or0, or1 = blocks_r[1] + blocks_r[3], blocks_r[1] - blocks_r[3]
        ei0, ei1 = blocks_i[0] + blocks_i[2], blocks_i[0] - blocks_i[2]
        oi0, oi1 = blocks_i[1] + blocks_i[3], blocks_i[1] - blocks_i[3]
        mixed.append(
            (
                (er0 + or0, ei0 + oi0),
                (er1 + oi1, ei1 - or1),
                (er0 - or0, ei0 - oi0),
                (er1 - oi1, ei1 + or1),
            )
        )
    for rest in range(RADIX):
        real = jnp.concatenate([mixed[0][rest][0], mixed[1][rest][0]], axis=1)
        imag = jnp.concatenate([mixed[0][rest][1], mixed[1][rest][1]], axis=1)
        value = jnp.concatenate([real, imag], axis=0)
        result = table_times((mq_ref[rest, 0], mq_ref[rest, 1]), value)
        for comp in (0, 1):
            row = ((first + comp) * RADIX + rest) * 2
            lanes = slice(128 * comp, 128 * comp + 128)
            out_ref[pl.ds(row, 128, stride=ROWS), :] = result[:128, lanes]
            out_ref[pl.ds(row + 1, 128, stride=ROWS), :] = result[128:, lanes]


XTILES = N // TILE


def even_body(p_ref, lame_in, shear_in, strain_ref, txf_ref, mq_ref, out_ref, odd_ref, scratch):
    step = pl.program_id(0)

    @pl.when(step < XTILES)
    def _():
        order = p_ref[...]
        scale = order * order * (3.0 - 2.0 * order) + residual_stiff
        shear_now = 2.0 * (scale * shear_in[...])
        lame_now = scale * lame_in[...]
        spread = lame_now * (strain_ref[0] + strain_ref[1] + strain_ref[2])
        where = pl.ds(pl.multiple_of(step * TILE, TILE), TILE)
        for comp in range(COMPS):
            part = shear_now * strain_ref[comp]
            if comp < 3:
                part = part + spread
            odd_ref[comp] = part[:, :HALF] - part[:, HALF:]
            folded = part[:, :HALF] + part[:, HALF:]
            scratch[comp, where, :] = times_table(folded, (txf_ref[0, 0], txf_ref[0, 1]))

    @pl.when(step == XTILES)
    def _():
        for pair in range(3):
            forward_y(scratch, mq_ref, out_ref, pair)


def forward_even(order, lame, shear, strain, txf, mq):
    last = XTILES - 1
    block = pl.BlockSpec((TILE, N), lambda i: (jnp.minimum(i, last), 0))
    return pl.pallas_call(
        even_body,
        grid=(XTILES + 1,),
        in_specs=[
            block,
            block,
            block,
            pl.BlockSpec((COMPS, TILE, N), lambda i: (0, jnp.minimum(i, last), 0)),
            pl.BlockSpec((1, 2, HALF, HALF), lambda i: (0, 0, 0, 0)),
            pl.BlockSpec((4, 2, HALF, HALF), lambda i: (0, 0, 0, 0)),
        ],
        out_specs=[
            pl.BlockSpec((BLOCK, LANE), lambda i: (0, 0)),
            pl.BlockSpec((COMPS, TILE, HALF), lambda i: (0, jnp.minimum(i, last), 0)),
        ],
        out_shape=[
            jax.ShapeDtypeStruct((BLOCK, LANE), f32),
            jax.ShapeDtypeStruct((COMPS, N, HALF), f32),
        ],
        scratch_shapes=[pltpu.VMEM((COMPS, N, HALF), f32)],
        compiler_params=params(),
        name="forward_even",
    )(order, lame, shear, strain, txf, mq)


def odd_body(odd_ref, txf_ref, mq_ref, out_ref, scratch):
    for comp in (0, 1):
        scratch[comp] = times_table(odd_ref[comp], (txf_ref[0, 0], txf_ref[0, 1]))
    pair = pl.program_id(0)
    first = pair * 2
    mixed = []
    for comp in (0, 1):
        blocks_r = [scratch[comp, pl.ds(128 * j, 128), pl.ds(0, 128)] for j in range(4)]
        blocks_i = [scratch[comp, pl.ds(128 * j, 128), pl.ds(128, 128)] for j in range(4)]
        er0, er1 = blocks_r[0] + blocks_r[2], blocks_r[0] - blocks_r[2]
        or0, or1 = blocks_r[1] + blocks_r[3], blocks_r[1] - blocks_r[3]
        ei0, ei1 = blocks_i[0] + blocks_i[2], blocks_i[0] - blocks_i[2]
        oi0, oi1 = blocks_i[1] + blocks_i[3], blocks_i[1] - blocks_i[3]
        mixed.append(
            (
                (er0 + or0, ei0 + oi0),
                (er1 + oi1, ei1 - or1),
                (er0 - or0, ei0 - oi0),
                (er1 - oi1, ei1 + or1),
            )
        )
    for rest in range(RADIX):
        real = jnp.concatenate([mixed[0][rest][0], mixed[1][rest][0]], axis=1)
        imag = jnp.concatenate([mixed[0][rest][1], mixed[1][rest][1]], axis=1)
        value = jnp.concatenate([real, imag], axis=0)
        result = table_times((mq_ref[rest, 0], mq_ref[rest, 1]), value)
        for comp in (0, 1):
            row = ((first + comp) * RADIX + rest) * 2
            lanes = slice(128 * comp, 128 * comp + 128)
            out_ref[pl.ds(row, 128, stride=ROWS), :] = result[:128, lanes]
            out_ref[pl.ds(row + 1, 128, stride=ROWS), :] = result[128:, lanes]


def forward_odd(odd, txf, mq):
    return pl.pallas_call(
        odd_body,
        grid=(3,),
        in_specs=[
            pl.BlockSpec((2, N, HALF), lambda i: (i, 0, 0)),
            pl.BlockSpec((1, 2, HALF, HALF), lambda i: (1, 0, 0, 0)),
            pl.BlockSpec((4, 2, HALF, HALF), lambda i: (0, 0, 0, 0)),
        ],
        out_specs=pl.BlockSpec((BLOCK, LANE), lambda i: (0, 0)),
        out_shape=jax.ShapeDtypeStruct((BLOCK, LANE), f32),
        scratch_shapes=[pltpu.VMEM((2, N, HALF), f32)],
        compiler_params=params(),
        name="forward_odd",
    )(odd, txf, mq)


def middle_body(band_ref, in_ref, mz_ref, out_ref, *, parity):
    rest = pl.program_id(0)
    forward = (mz_ref[0, 0], mz_ref[0, 1])
    backward = (mz_ref[1, 0], mz_ref[1, 1])
    tau_r, tau_i = [], []
    for pair in range(3):
        reals, imags = [], []
        for comp in (0, 1):
            row = (pair * 2 + comp) * RADIX * 2 + rest * 2
            reals.append(in_ref[pl.ds(row, 128, stride=ROWS), :])
            imags.append(in_ref[pl.ds(row + 1, 128, stride=ROWS), :])
        value = jnp.concatenate(
            [jnp.concatenate(reals, axis=1), jnp.concatenate(imags, axis=1)], axis=0
        )
        result = table_times(forward, value)
        for comp in (0, 1):
            lanes = slice(128 * comp, 128 * comp + 128)
            tau_r.append(result[:128, lanes])
            tau_i.append(result[128:, lanes])
    shape = (DEPTH, LANE)
    depth_index = lax.broadcasted_iota(jnp.int32, shape, 0)
    xi_z = jnp.where(depth_index < DEPTH // 2, depth_index, depth_index - DEPTH).astype(f32)
    xi_x = (2 * lax.broadcasted_iota(jnp.int32, shape, 1) + parity).astype(f32)
    wave_y = band_ref[0] * RADIX + rest
    xi_y = jnp.where(wave_y < N // 2, wave_y, wave_y - N).astype(f32)
    wave_sq = xi_x * xi_x + xi_y * xi_y + xi_z * xi_z
    live = (wave_sq > 0.5) & (xi_x < float(HALF))
    safe = jnp.where(live, wave_sq, 1.0)
    inverse = 1.0 / safe
    first = jnp.where(live, (0.5 / shear_ref) * inverse, 0.0)
    second = jnp.where(live, (0.5 * coupling) * (inverse * inverse), 0.0)
    grids = []
    for tau in (tau_r, tau_i):
        t_xx, t_yy, t_zz, t_yz, t_xz, t_xy = tau
        v_x = t_xx * xi_x + t_xy * xi_y + t_xz * xi_z
        v_y = t_xy * xi_x + t_yy * xi_y + t_yz * xi_z
        v_z = t_xz * xi_x + t_yz * xi_y + t_zz * xi_z
        inner = (xi_x * v_x + xi_y * v_y + xi_z * v_z) * second
        h_x = v_x * first - xi_x * inner
        h_y = v_y * first - xi_y * inner
        h_z = v_z * first - xi_z * inner
        grids.append(
            (
                2.0 * xi_x * h_x,
                2.0 * xi_y * h_y,
                2.0 * xi_z * h_z,
                xi_z * h_y + xi_y * h_z,
                xi_z * h_x + xi_x * h_z,
                xi_y * h_x + xi_x * h_y,
            )
        )
    for pair in range(3):
        real = jnp.concatenate([grids[0][pair * 2], grids[0][pair * 2 + 1]], axis=1)
        imag = jnp.concatenate([grids[1][pair * 2], grids[1][pair * 2 + 1]], axis=1)
        result = table_times(backward, jnp.concatenate([real, imag], axis=0))
        for comp in (0, 1):
            row = (pair * 2 + comp) * RADIX * 2 + rest * 2
            lanes = slice(128 * comp, 128 * comp + 128)
            out_ref[pl.ds(row, 128, stride=ROWS), :] = result[:128, lanes]
            out_ref[pl.ds(row + 1, 128, stride=ROWS), :] = result[128:, lanes]


def middle(band, received, mz, parity):
    return pl.pallas_call(
        functools.partial(middle_body, parity=parity),
        grid=(RADIX,),
        in_specs=[
            pl.BlockSpec(memory_space=pltpu.SMEM),
            pl.BlockSpec((BLOCK, LANE), lambda i: (0, 0)),
            pl.BlockSpec((2, 2, HALF, HALF), lambda i: (0, 0, 0, 0)),
        ],
        out_specs=pl.BlockSpec((BLOCK, LANE), lambda i: (0, 0)),
        out_shape=jax.ShapeDtypeStruct((BLOCK, LANE), f32),
        compiler_params=params(),
        name="middle_even" if parity == 0 else "middle_odd",
    )(band, received, mz)


def inverse_y(in_ref, mqi_ref, pair):
    blocks = []
    for rest in range(RADIX):
        reals, imags = [], []
        for comp in (0, 1):
            row = (pair * 2 + comp) * RADIX * 2 + rest * 2
            reals.append(in_ref[pl.ds(row, 128, stride=ROWS), :])
            imags.append(in_ref[pl.ds(row + 1, 128, stride=ROWS), :])
        value = jnp.concatenate(
            [jnp.concatenate(reals, axis=1), jnp.concatenate(imags, axis=1)], axis=0
        )
        result = table_times((mqi_ref[rest, 0], mqi_ref[rest, 1]), value)
        blocks.append((result[:128], result[128:]))
    er0, er1 = blocks[0][0] + blocks[2][0], blocks[0][0] - blocks[2][0]
    ei0, ei1 = blocks[0][1] + blocks[2][1], blocks[0][1] - blocks[2][1]
    or0, or1 = blocks[1][0] + blocks[3][0], blocks[1][0] - blocks[3][0]
    oi0, oi1 = blocks[1][1] + blocks[3][1], blocks[1][1] - blocks[3][1]
    return (
        (er0 + or0, ei0 + oi0),
        (er1 - oi1, ei1 + or1),
        (er0 - or0, ei0 - oi0),
        (er1 + oi1, ei1 - or1),
    )


def inverse_even_body(in_ref, mqi_ref, txi_ref, out_ref):
    table = (txi_ref[0, 0], txi_ref[0, 1])
    planes = inverse_y(in_ref, mqi_ref, pl.program_id(0))
    for comp in (0, 1):
        lanes = slice(128 * comp, 128 * comp + 128)
        for j in range(RADIX):
            value = jnp.concatenate([planes[j][0][:, lanes], planes[j][1][:, lanes]], axis=1)
            out_ref[comp, pl.ds(128 * j, 128), :] = times_table(value, table)


def inverse_odd_body(in_ref, even_ref, strain_ref, mqi_ref, txi_ref, out_ref):
    table = (txi_ref[0, 0], txi_ref[0, 1])
    planes = inverse_y(in_ref, mqi_ref, pl.program_id(0))
    for comp in (0, 1):
        lanes = slice(128 * comp, 128 * comp + 128)
        for j in range(RADIX):
            value = jnp.concatenate([planes[j][0][:, lanes], planes[j][1][:, lanes]], axis=1)
            odd = times_table(value, table)
            where = pl.ds(128 * j, 128)
            even = even_ref[comp, where, :]
            left = pl.ds(0, HALF)
            right = pl.ds(HALF, HALF)
            out_ref[comp, where, left] = strain_ref[comp, where, left] - (even + odd)
            out_ref[comp, where, right] = strain_ref[comp, where, right] - (even - odd)


def inverse_even(returned, mqi, txi):
    return pl.pallas_call(
        inverse_even_body,
        grid=(3,),
        in_specs=[
            pl.BlockSpec((BLOCK, LANE), lambda i: (0, 0)),
            pl.BlockSpec((4, 2, HALF, HALF), lambda i: (0, 0, 0, 0)),
            pl.BlockSpec((1, 2, HALF, HALF), lambda i: (0, 0, 0, 0)),
        ],
        out_specs=pl.BlockSpec((2, N, HALF), lambda i: (i, 0, 0)),
        out_shape=jax.ShapeDtypeStruct((COMPS, N, HALF), f32),
        compiler_params=params(),
        name="inverse_even",
    )(returned, mqi, txi)


def inverse_odd(returned, even, strain, mqi, txi):
    return pl.pallas_call(
        inverse_odd_body,
        grid=(3,),
        in_specs=[
            pl.BlockSpec((BLOCK, LANE), lambda i: (0, 0)),
            pl.BlockSpec((2, N, HALF), lambda i: (i, 0, 0)),
            pl.BlockSpec((2, N, N), lambda i: (i, 0, 0)),
            pl.BlockSpec((4, 2, HALF, HALF), lambda i: (0, 0, 0, 0)),
            pl.BlockSpec((1, 2, HALF, HALF), lambda i: (1, 0, 0, 0)),
        ],
        out_specs=pl.BlockSpec((2, N, N), lambda i: (i, 0, 0)),
        out_shape=jax.ShapeDtypeStruct((COMPS, N, N), f32),
        compiler_params=params(),
        name="inverse_odd",
    )(returned, even, strain, mqi, txi)


def exchange(block):
    packed = block.reshape(DEPTH, ROWS, LANE)
    moved = lax.all_to_all(packed, "gz", split_axis=0, concat_axis=0, tiled=True)
    return moved.reshape(BLOCK, LANE)


def neighbours(plane, count):
    ahead = [(i, (i + 1) % count) for i in range(count)]
    behind = [((i + 1) % count, i) for i in range(count)]
    return lax.ppermute(plane, "gz", ahead), lax.ppermute(plane, "gz", behind)


def shards(
    order_param,
    concentration,
    strain,
    grain_ids,
    seed_labels,
    grain_moduli,
    grain_mobility,
    seed_rate,
):
    count = lax.axis_size("gz")
    order_now = order_param.reshape(N, N)
    conc_now = concentration.reshape(N, N)
    planes = strain.reshape(COMPS, N, N)
    txf, mq, mz, mqi, txi = make_tables()
    lame, shear, kinetic, decay = coefficients(
        grain_moduli,
        grain_mobility,
        seed_rate,
        grain_ids.reshape(N, N),
        seed_labels.reshape(N, N),
        planes,
    )
    for _ in range(SUBSTEPS):
        halos = neighbours(order_now, count) + neighbours(conc_now, count)
        order_now, conc_now = substep(order_now, conc_now, halos, kinetic, decay)
    band = lax.axis_index("gz").astype(jnp.int32).reshape(1)
    even, odd = forward_even(order_now, lame, shear, planes, txf, mq)
    even = exchange(even)
    odd = exchange(forward_odd(odd, txf, mq))
    even = exchange(middle(band, even, mz, 0))
    odd = exchange(middle(band, odd, mz, 1))
    partial = inverse_even(even, mqi, txi)
    strain_next = inverse_odd(odd, partial, planes, mqi, txi)
    return (
        order_now.reshape(1, N, N),
        conc_now.reshape(1, N, N),
        strain_next.reshape(COMPS, 1, N, N),
    )


def solution(mesh):
    return jax.shard_map(
        shards,
        mesh=mesh,
        in_specs=(
            P("gz", None, None),
            P("gz", None, None),
            P(None, "gz", None, None),
            P("gz", None, None),
            P("gz", None, None),
            P(),
            P(),
            P(),
        ),
        out_specs=(P("gz", None, None), P("gz", None, None), P(None, "gz", None, None)),
        check_vma=False,
    )
```

```python
import functools
import math

import jax
import jax.numpy as jnp
from jax import lax
from jax.experimental import pallas as pl
from jax.experimental.pallas import tpu as pltpu
from jax.sharding import PartitionSpec as P

SUBSTEPS = 2
N = 512
HALF = 256
LANE = 128
DEPTH = 128
COMPS = 6
RADIX = 4
PAIRS = COMPS // 2
SUB = 8
QROWS = PAIRS * SUB
PROWS = RADIX * SUB
ROWS = PAIRS * RADIX * SUB

time_step = 0.05
grad_coef = 1.0
well_height = 1.0
drive_coef = 2.0
conc_eq = 0.5
mech_boost = 1.0
diffusivity = 1.0
release_coef = 1.0
residual_stiff = 0.1
lame_ref = 1.0
shear_ref = 1.0
coupling = (lame_ref + shear_ref) / (shear_ref * (lame_ref + 2.0 * shear_ref))

f32 = jnp.float32
bf16 = jnp.bfloat16
VMEM_LIMIT = 40 * 1024 * 1024


def params(dims=1):
    return pltpu.CompilerParams(
        dimension_semantics=("arbitrary",) * dims, vmem_limit_bytes=VMEM_LIMIT
    )


def split(value):
    high = value.astype(bf16)
    low = (value - high.astype(f32)).astype(bf16)
    return high, low


def mul(left, right):
    return lax.dot_general(
        left, right, (((1,), (0,)), ((), ())), preferred_element_type=f32
    )


def table_times(table, value):
    high, low = split(value)
    return mul(table[0], high) + mul(table[0], low) + mul(table[1], high)


def times_table(value, table):
    high, low = split(value)
    return mul(high, table[0]) + mul(low, table[0]) + mul(high, table[1])


def unit_cos(index):
    wrapped = ((index + 256) & 511) - 256
    angle = (128 - jnp.abs(wrapped)).astype(f32) * (2.0 * math.pi / 512.0)
    square = angle * angle
    poly = 1.0 / 6227020800.0
    for power in (39916800.0, 362880.0, 5040.0, 120.0, 6.0):
        poly = 1.0 / power - square * poly
    return angle * (1.0 - square * poly)


def table_body(txf_ref, mq_ref, mz_ref, mqi_ref, txi_ref):
    rows = lax.broadcasted_iota(jnp.int32, (HALF, HALF), 0)
    cols = lax.broadcasted_iota(jnp.int32, (HALF, HALF), 1)
    row_low = rows & 127
    row_top = rows >> 7
    col_low = cols & 127
    col_top = cols >> 7

    def put(ref, slot, value):
        high, low = split(value)
        ref[slot, 0] = high
        ref[slot, 1] = low

    turn = (row_top - col_top) * 128
    for parity in range(2):
        wave = 2 * col_low + parity
        put(txf_ref, parity, unit_cos(rows * wave + col_top * 128))
        wave = 2 * row_low + parity
        weight = jnp.where(wave == 0, 1.0, 2.0) * (1.0 / float(N * N * DEPTH))
        put(txi_ref, parity, unit_cos(wave * cols + row_top * 128) * weight)
    for rest in range(RADIX):
        put(mq_ref, rest, unit_cos((4 * row_low + rest) * col_low + turn))
        put(mqi_ref, rest, unit_cos((4 * col_low + rest) * row_low - turn))
    put(mz_ref, 0, unit_cos(4 * row_low * col_low + turn))
    put(mz_ref, 1, unit_cos(4 * row_low * col_low - turn))


def make_tables():
    shape = lambda count: jax.ShapeDtypeStruct((count, 2, HALF, HALF), bf16)
    return pl.pallas_call(
        table_body,
        out_shape=(shape(2), shape(4), shape(2), shape(4), shape(2)),
        compiler_params=pltpu.CompilerParams(vmem_limit_bytes=VMEM_LIMIT),
        name="tables",
    )()


TILE = 128
STRIP = 16


def strips(rows, body):
    def step(index, carry):
        body(pl.multiple_of(index * STRIP, STRIP))
        return carry

    lax.fori_loop(0, rows // STRIP, step, 0)


def lane_table(read, count):
    lanes = lax.broadcasted_iota(jnp.int32, (STRIP, LANE), 1)
    table = jnp.zeros((STRIP, LANE), f32)
    for index in range(count):
        table = jnp.where(lanes == index, read(index), table)
    return table


def pick(table, index):
    parts = [
        jnp.take_along_axis(table, index[:, LANE * k : LANE * (k + 1)], axis=1)
        for k in range(N // LANE)
    ]
    return jnp.concatenate(parts, axis=1)


def coef_body(moduli, mobility, rates, grain_ref, label_ref, strain_ref, lame_out, shear_out, kin_out, dec_out):
    grains = mobility.shape[0]
    lames = lane_table(lambda k: moduli[0, k], grains)
    shears = lane_table(lambda k: moduli[1, k], grains)
    mobs = lane_table(lambda k: mobility[k], grains)
    speeds = lane_table(lambda k: rates[k - 1] if k else 0.0, rates.shape[0] + 1)

    def strip(start):
        where = pl.ds(start, STRIP)
        grain = grain_ref[where, :]
        lame = pick(lames, grain)
        shear = pick(shears, grain)
        parts = [strain_ref[comp, where, :] for comp in range(COMPS)]
        trace = parts[0] + parts[1] + parts[2]
        square = (
            parts[0] * parts[0]
            + parts[1] * parts[1]
            + parts[2] * parts[2]
            + 2.0 * (parts[3] * parts[3] + parts[4] * parts[4] + parts[5] * parts[5])
        )
        energy = 0.5 * lame * trace * trace + shear * square
        mech = 1.0 + mech_boost * energy / (1.0 + energy)
        lame_out[where, :] = lame
        shear_out[where, :] = shear
        kin_out[where, :] = time_step * pick(mobs, grain) * mech
        dec_out[where, :] = time_step * pick(speeds, label_ref[where, :])

    strips(TILE, strip)


PLANE = jax.ShapeDtypeStruct((N, N), f32)
WHOLE = pl.BlockSpec((N, N), lambda i: (0, 0))
STRIPE = pl.BlockSpec((TILE, N), lambda i: (i, 0))


def coefficients(moduli, mobility, rates, grain, label, strain):
    smem = pl.BlockSpec(memory_space=pltpu.SMEM)
    return pl.pallas_call(
        coef_body,
        grid=(N // TILE,),
        in_specs=[smem, smem, smem, STRIPE, STRIPE, pl.BlockSpec((COMPS, TILE, N), lambda i: (0, i, 0))],
        out_specs=[STRIPE] * 4,
        out_shape=[PLANE] * 4,
        compiler_params=params(),
        name="coefficients",
    )(moduli, mobility, rates, grain, label, strain)


def planar_sum(ref, start):
    center = ref[pl.ds(start, STRIP), :]
    before = ref[pl.ds(pl.multiple_of((start + N - 8) & (N - 1), 8), 8), :]
    after = ref[pl.ds(pl.multiple_of((start + STRIP) & (N - 1), 8), 8), :]
    tall = jnp.concatenate([before, center, after], axis=0)
    height = STRIP + 16
    above = pltpu.roll(tall, 1, 0)[8 : 8 + STRIP]
    below = pltpu.roll(tall, height - 1, 0)[8 : 8 + STRIP]
    sides = pltpu.roll(center, 1, 1) + pltpu.roll(center, N - 1, 1)
    return center, (above + below) + sides


def next_order(p_ref, start, halo_sum, conc_now, kinetic, decay):
    order_now, order_sum = planar_sum(p_ref, start)
    lap_order = order_sum + halo_sum - 6.0 * order_now
    slope = order_now * (1.0 - order_now)
    well_grad = 2.0 * slope * (1.0 - 2.0 * order_now)
    force = (
        grad_coef * lap_order
        - well_height * well_grad
        + drive_coef * 6.0 * slope * (conc_now - conc_eq)
    )
    return order_now + kinetic * force - decay * order_now


def order_body(p_ref, c_ref, up_ref, down_ref, kin_ref, dec_ref, p_out):
    base = pl.program_id(0) * TILE

    def strip(local):
        where = pl.ds(local, STRIP)
        start = pl.multiple_of(base + local, STRIP)
        p_out[where, :] = next_order(
            p_ref,
            start,
            up_ref[where, :] + down_ref[where, :],
            c_ref[where, :],
            kin_ref[where, :],
            dec_ref[where, :],
        )

    strips(TILE, strip)


def order_step(order_now, conc_now, halos, kinetic, decay):
    return pl.pallas_call(
        order_body,
        grid=(N // TILE,),
        in_specs=[WHOLE] + [STRIPE] * 5,
        out_specs=STRIPE,
        out_shape=PLANE,
        compiler_params=params(),
        name="order_step",
    )(order_now, conc_now, *halos, kinetic, decay)


def conc_body(c_ref, p_ref, new_ref, up_ref, down_ref, c_out):
    base = pl.program_id(0) * TILE

    def strip(local):
        where = pl.ds(local, STRIP)
        conc_now, conc_sum = planar_sum(c_ref, pl.multiple_of(base + local, STRIP))
        lap_conc = conc_sum + (up_ref[where, :] + down_ref[where, :]) - 6.0 * conc_now
        c_out[where, :] = (
            conc_now
            + time_step * diffusivity * lap_conc
            + release_coef * (p_ref[where, :] - new_ref[where, :])
        )

    strips(TILE, strip)


def conc_step(conc_now, order_now, order_new, halos):
    return pl.pallas_call(
        conc_body,
        grid=(N // TILE,),
        in_specs=[WHOLE] + [STRIPE] * 4,
        out_specs=STRIPE,
        out_shape=PLANE,
        compiler_params=params(),
        name="conc_step",
    )(conc_now, order_now, order_new, *halos)


XTILES = N // TILE


def fold_blocks(scratch, comp, lanes_r, lanes_i, rest):
    reals = [scratch[comp, pl.ds(128 * j, 128), lanes_r] for j in range(RADIX)]
    imags = [scratch[comp, pl.ds(128 * j, 128), lanes_i] for j in range(RADIX)]
    if rest % 2 == 0:
        sign = 1.0 if rest == 0 else -1.0
        real = (reals[0] + reals[2]) + sign * (reals[1] + reals[3])
        imag = (imags[0] + imags[2]) + sign * (imags[1] + imags[3])
    elif rest == 1:
        real = (reals[0] - reals[2]) + (imags[1] - imags[3])
        imag = (imags[0] - imags[2]) - (reals[1] - reals[3])
    else:
        real = (reals[0] - reals[2]) - (imags[1] - imags[3])
        imag = (imags[0] - imags[2]) + (reals[1] - reals[3])
    return real, imag


def forward_body(
    p_ref, c_ref, up_ref, down_ref, kin_ref, dec_ref, lame_in, shear_in, strain_ref,
    txf_ref, mq_ref, out_ref, p_out, scratch,
):
    step = pl.program_id(0)

    @pl.when(step < XTILES)
    def _():
        base = step * TILE

        def strip(local):
            where = pl.ds(local, STRIP)
            p_out[where, :] = next_order(
                p_ref,
                pl.multiple_of(base + local, STRIP),
                up_ref[where, :] + down_ref[where, :],
                c_ref[where, :],
                kin_ref[where, :],
                dec_ref[where, :],
            )

        strips(TILE, strip)
        order = p_out[...]
        scale = order * order * (3.0 - 2.0 * order) + residual_stiff
        shear_now = 2.0 * (scale * shear_in[...])
        lame_now = scale * lame_in[...]
        spread = lame_now * (strain_ref[0] + strain_ref[1] + strain_ref[2])
        rows = pl.ds(pl.multiple_of(base, TILE), TILE)
        for comp in range(COMPS):
            part = shear_now * strain_ref[comp]
            if comp < 3:
                part = part + spread
            left = part[:, :HALF]
            right = part[:, HALF:]
            for parity, folded in ((0, left + right), (1, left - right)):
                table = (txf_ref[parity, 0], txf_ref[parity, 1])
                scratch[comp, rows, pl.ds(HALF * parity, HALF)] = times_table(folded, table)

    for rest in range(RADIX):

        @pl.when(step == XTILES + rest)
        def _():
            out = out_ref.reshape(LANE * QROWS, LANE)
            table = (mq_ref[rest, 0], mq_ref[rest, 1])
            for pair in range(PAIRS):
                for parity in range(2):
                    lanes_r = pl.ds(HALF * parity, LANE)
                    lanes_i = pl.ds(HALF * parity + LANE, LANE)
                    both = [
                        fold_blocks(scratch, 2 * pair + k, lanes_r, lanes_i, rest) for k in (0, 1)
                    ]
                    real = jnp.concatenate([both[0][0], both[1][0]], axis=1)
                    imag = jnp.concatenate([both[0][1], both[1][1]], axis=1)
                    result = table_times(table, jnp.concatenate([real, imag], axis=0))
                    row = pair * SUB + parity * 4
                    for k in (0, 1):
                        lanes = slice(LANE * k, LANE * (k + 1))
                        out[pl.ds(row + 2 * k, LANE, stride=QROWS), :] = result[:LANE, lanes]
                        out[pl.ds(row + 2 * k + 1, LANE, stride=QROWS), :] = result[LANE:, lanes]


BUFFER = jax.ShapeDtypeStruct((LANE, PAIRS, RADIX, SUB, LANE), f32)
REST_BLOCK = (LANE, PAIRS, None, SUB, LANE)
PAIR_BLOCK = (LANE, None, RADIX, SUB, LANE)


def full(*shape):
    return pl.BlockSpec(shape, lambda i: (0,) * len(shape))


def forward(order, conc, halos, kinetic, decay, lame, shear, strain, txf, mq):
    last = XTILES - 1
    stripe = pl.BlockSpec((TILE, N), lambda i: (jnp.minimum(i, last), 0))
    return pl.pallas_call(
        forward_body,
        grid=(XTILES + RADIX,),
        in_specs=[
            full(N, N),
            stripe,
            stripe,
            stripe,
            stripe,
            stripe,
            stripe,
            stripe,
            pl.BlockSpec((COMPS, TILE, N), lambda i: (0, jnp.minimum(i, last), 0)),
            full(2, 2, HALF, HALF),
            full(4, 2, HALF, HALF),
        ],
        out_specs=[
            pl.BlockSpec(REST_BLOCK, lambda i: (0, 0, jnp.maximum(i - XTILES, 0), 0, 0)),
            stripe,
        ],
        out_shape=[BUFFER, PLANE],
        scratch_shapes=[pltpu.VMEM((COMPS, N, N), f32)],
        compiler_params=params(),
        name="forward",
    )(order, conc, *halos, kinetic, decay, lame, shear, strain, txf, mq)


def take_pair(ref, row, stride):
    reals, imags = [], []
    for k in (0, 1):
        reals.append(ref[pl.ds(row + 2 * k, LANE, stride=stride), :])
        imags.append(ref[pl.ds(row + 2 * k + 1, LANE, stride=stride), :])
    return jnp.concatenate(
        [jnp.concatenate(reals, axis=1), jnp.concatenate(imags, axis=1)], axis=0
    )


def middle_body(band_ref, in_ref, mz_ref, out_ref):
    rest = pl.program_id(0)
    source = in_ref.reshape(LANE * QROWS, LANE)
    out = out_ref.reshape(LANE * QROWS, LANE)
    onward = (mz_ref[0, 0], mz_ref[0, 1])
    backward = (mz_ref[1, 0], mz_ref[1, 1])
    shape = (DEPTH, LANE)
    depth_index = lax.broadcasted_iota(jnp.int32, shape, 0)
    xi_z = jnp.where(depth_index < DEPTH // 2, depth_index, depth_index - DEPTH).astype(f32)
    wave_y = band_ref[0] * RADIX + rest
    xi_y = jnp.where(wave_y < N // 2, wave_y, wave_y - N).astype(f32)
    for parity in range(2):
        tau_r, tau_i = [], []
        for pair in range(PAIRS):
            result = table_times(onward, take_pair(source, pair * SUB + parity * 4, QROWS))
            for k in (0, 1):
                lanes = slice(LANE * k, LANE * (k + 1))
                tau_r.append(result[:LANE, lanes])
                tau_i.append(result[LANE:, lanes])
        xi_x = (2 * lax.broadcasted_iota(jnp.int32, shape, 1) + parity).astype(f32)
        wave_sq = xi_x * xi_x + xi_y * xi_y + xi_z * xi_z
        live = (wave_sq > 0.5) & (xi_x < float(HALF))
        safe = jnp.where(live, wave_sq, 1.0)
        inverse = 1.0 / safe
        first = jnp.where(live, (0.5 / shear_ref) * inverse, 0.0)
        second = jnp.where(live, (0.5 * coupling) * (inverse * inverse), 0.0)
        grids = []
        for tau in (tau_r, tau_i):
            t_xx, t_yy, t_zz, t_yz, t_xz, t_xy = tau
            v_x = t_xx * xi_x + t_xy * xi_y + t_xz * xi_z
            v_y = t_xy * xi_x + t_yy * xi_y + t_yz * xi_z
            v_z = t_xz * xi_x + t_yz * xi_y + t_zz * xi_z
            inner = (xi_x * v_x + xi_y * v_y + xi_z * v_z) * second
            h_x = v_x * first - xi_x * inner
            h_y = v_y * first - xi_y * inner
            h_z = v_z * first - xi_z * inner
            grids.append(
                (
                    2.0 * xi_x * h_x,
                    2.0 * xi_y * h_y,
                    2.0 * xi_z * h_z,
                    xi_z * h_y + xi_y * h_z,
                    xi_z * h_x + xi_x * h_z,
                    xi_y * h_x + xi_x * h_y,
                )
            )
        for pair in range(PAIRS):
            real = jnp.concatenate([grids[0][pair * 2], grids[0][pair * 2 + 1]], axis=1)
            imag = jnp.concatenate([grids[1][pair * 2], grids[1][pair * 2 + 1]], axis=1)
            result = table_times(backward, jnp.concatenate([real, imag], axis=0))
            row = pair * SUB + parity * 4
            for k in (0, 1):
                lanes = slice(LANE * k, LANE * (k + 1))
                out[pl.ds(row + 2 * k, LANE, stride=QROWS), :] = result[:LANE, lanes]
                out[pl.ds(row + 2 * k + 1, LANE, stride=QROWS), :] = result[LANE:, lanes]


def middle(band, received, mz):
    spec = pl.BlockSpec(REST_BLOCK, lambda i: (0, 0, i, 0, 0))
    return pl.pallas_call(
        middle_body,
        grid=(RADIX,),
        in_specs=[pl.BlockSpec(memory_space=pltpu.SMEM), spec, full(2, 2, HALF, HALF)],
        out_specs=spec,
        out_shape=BUFFER,
        compiler_params=params(),
        name="middle",
    )(band, received, mz)


def inverse_y(source, mqi_ref, parity):
    blocks = []
    for rest in range(RADIX):
        value = take_pair(source, rest * SUB + parity * 4, PROWS)
        result = table_times((mqi_ref[rest, 0], mqi_ref[rest, 1]), value)
        blocks.append((result[:LANE], result[LANE:]))
    er0, er1 = blocks[0][0] + blocks[2][0], blocks[0][0] - blocks[2][0]
    ei0, ei1 = blocks[0][1] + blocks[2][1], blocks[0][1] - blocks[2][1]
    or0, or1 = blocks[1][0] + blocks[3][0], blocks[1][0] - blocks[3][0]
    oi0, oi1 = blocks[1][1] + blocks[3][1], blocks[1][1] - blocks[3][1]
    return (
        (er0 + or0, ei0 + oi0),
        (er1 - oi1, ei1 + or1),
        (er0 - or0, ei0 - oi0),
        (er1 + oi1, ei1 - or1),
    )


def inverse_body(in_ref, strain_ref, mqi_ref, txi_ref, out_ref):
    source = in_ref.reshape(LANE * PROWS, LANE)
    planes = [inverse_y(source, mqi_ref, parity) for parity in range(2)]
    for k in (0, 1):
        lanes = slice(LANE * k, LANE * (k + 1))
        for j in range(RADIX):
            halves = []
            for parity in range(2):
                real, imag = planes[parity][j]
                value = jnp.concatenate([real[:, lanes], imag[:, lanes]], axis=1)
                halves.append(times_table(value, (txi_ref[parity, 0], txi_ref[parity, 1])))
            even, odd = halves
            where = pl.ds(LANE * j, LANE)
            left = pl.ds(0, HALF)
            right = pl.ds(HALF, HALF)
            out_ref[k, where, left] = strain_ref[k, where, left] - (even + odd)
            out_ref[k, where, right] = strain_ref[k, where, right] - (even - odd)


def inverse(returned, strain, mqi, txi):
    return pl.pallas_call(
        inverse_body,
        grid=(PAIRS,),
        in_specs=[
            pl.BlockSpec(PAIR_BLOCK, lambda i: (0, i, 0, 0, 0)),
            pl.BlockSpec((2, N, N), lambda i: (i, 0, 0)),
            full(4, 2, HALF, HALF),
            full(2, 2, HALF, HALF),
        ],
        out_specs=pl.BlockSpec((2, N, N), lambda i: (i, 0, 0)),
        out_shape=jax.ShapeDtypeStruct((COMPS, N, N), f32),
        compiler_params=params(),
        name="inverse",
    )(returned, strain, mqi, txi)


def exchange(block):
    packed = block.reshape(DEPTH, ROWS, LANE)
    moved = lax.all_to_all(packed, "gz", split_axis=0, concat_axis=0, tiled=True)
    return moved.reshape(BUFFER.shape)


def neighbours(plane, count):
    ahead = [(i, (i + 1) % count) for i in range(count)]
    behind = [((i + 1) % count, i) for i in range(count)]
    return lax.ppermute(plane, "gz", ahead), lax.ppermute(plane, "gz", behind)


def shards(
    order_param,
    concentration,
    strain,
    grain_ids,
    seed_labels,
    grain_moduli,
    grain_mobility,
    seed_rate,
):
    count = lax.axis_size("gz")
    order_now = order_param.reshape(N, N)
    conc_now = concentration.reshape(N, N)
    planes = strain.reshape(COMPS, N, N)
    order_halos = neighbours(order_now, count)
    conc_halos = neighbours(conc_now, count)
    lame, shear, kinetic, decay = coefficients(
        grain_moduli,
        grain_mobility,
        seed_rate,
        grain_ids.reshape(N, N),
        seed_labels.reshape(N, N),
        planes,
    )
    txf, mq, mz, mqi, txi = make_tables()
    for _ in range(SUBSTEPS - 1):
        order_new = order_step(order_now, conc_now, order_halos, kinetic, decay)
        order_halos = neighbours(order_new, count)
        conc_new = conc_step(conc_now, order_now, order_new, conc_halos)
        conc_halos = neighbours(conc_new, count)
        order_now, conc_now = order_new, conc_new
    spectra, order_next = forward(
        order_now, conc_now, order_halos, kinetic, decay, lame, shear, planes, txf, mq
    )
    conc_next = conc_step(conc_now, order_now, order_next, conc_halos)
    band = lax.axis_index("gz").astype(jnp.int32).reshape(1)
    returned = exchange(middle(band, exchange(spectra), mz))
    strain_next = inverse(returned, planes, mqi, txi)
    return (
        order_next.reshape(1, N, N),
        conc_next.reshape(1, N, N),
        strain_next.reshape(COMPS, 1, N, N),
    )


def solution(mesh):
    return jax.shard_map(
        shards,
        mesh=mesh,
        in_specs=(
            P("gz", None, None),
            P("gz", None, None),
            P(None, "gz", None, None),
            P("gz", None, None),
            P("gz", None, None),
            P(),
            P(),
            P(),
        ),
        out_specs=(P("gz", None, None), P("gz", None, None), P(None, "gz", None, None)),
        check_vma=False,
    )
```

```python
import functools
import math

import jax
import jax.numpy as jnp
from jax import lax
from jax.experimental import pallas as pl
from jax.experimental.pallas import tpu as pltpu
from jax.sharding import PartitionSpec as P

SUBSTEPS = 2
N = 512
HALF = 256
LANE = 128
DEPTH = 128
COMPS = 6
RADIX = 4
PAIRS = COMPS // 2
SUB = 8
BLOCKS = PAIRS * RADIX
ROWS = BLOCKS * SUB
PITCH = (BLOCKS + 1) * SUB

time_step = 0.05
grad_coef = 1.0
well_height = 1.0
drive_coef = 2.0
conc_eq = 0.5
mech_boost = 1.0
diffusivity = 1.0
release_coef = 1.0
residual_stiff = 0.1
lame_ref = 1.0
shear_ref = 1.0
coupling = (lame_ref + shear_ref) / (shear_ref * (lame_ref + 2.0 * shear_ref))

f32 = jnp.float32
bf16 = jnp.bfloat16
MIB = 1024 * 1024


def params(mib, dims=0):
    semantics = ("arbitrary",) * dims if dims else None
    return pltpu.CompilerParams(dimension_semantics=semantics, vmem_limit_bytes=mib * MIB)


def in_hbm(value):
    return pltpu.with_memory_space_constraint(value, pltpu.HBM)


RESIDENT = pl.BlockSpec(memory_space=pltpu.VMEM)
REMAIN = pl.BlockSpec(memory_space=pl.ANY)
SCALAR = pl.BlockSpec(memory_space=pltpu.SMEM)


def split(value):
    high = value.astype(bf16)
    low = (value - high.astype(f32)).astype(bf16)
    return high, low


def mul(left, right):
    return lax.dot_general(
        left, right, (((1,), (0,)), ((), ())), preferred_element_type=f32
    )


def table_times(table, value):
    high, low = split(value)
    return mul(table[0], high) + mul(table[0], low) + mul(table[1], high)


def times_table(value, table):
    high, low = split(value)
    return mul(high, table[0]) + mul(low, table[0]) + mul(high, table[1])


def unit_cos(index):
    wrapped = ((index + 256) & 511) - 256
    angle = (128 - jnp.abs(wrapped)).astype(f32) * (2.0 * math.pi / 512.0)
    square = angle * angle
    poly = 1.0 / 6227020800.0
    for power in (39916800.0, 362880.0, 5040.0, 120.0, 6.0):
        poly = 1.0 / power - square * poly
    return angle * (1.0 - square * poly)


def table_grid():
    rows = lax.broadcasted_iota(jnp.int32, (HALF, HALF), 0)
    cols = lax.broadcasted_iota(jnp.int32, (HALF, HALF), 1)
    turn = ((rows >> 7) - (cols >> 7)) * 128
    return rows, cols, rows & 127, cols & 127, turn


def put(ref, slot, value):
    high, low = split(value)
    ref[slot, 0] = high
    ref[slot, 1] = low


def onward_body(order_ref, txf_ref, mq_ref):
    rows, cols, row_low, col_low, turn = table_grid()
    for parity in range(2):
        wave = 2 * col_low + parity
        put(txf_ref, parity, unit_cos(rows * wave + (cols >> 7) * 128))
    for rest in range(RADIX):
        put(mq_ref, rest, unit_cos((4 * row_low + rest) * col_low + turn))


def backward_body(order_ref, mz_ref, mqi_ref, txi_ref):
    rows, cols, row_low, col_low, turn = table_grid()
    for parity in range(2):
        wave = 2 * row_low + parity
        weight = jnp.where(wave == 0, 1.0, 2.0) * (1.0 / float(N * N * DEPTH))
        put(txi_ref, parity, unit_cos(wave * cols + (rows >> 7) * 128) * weight)
    for rest in range(RADIX):
        put(mqi_ref, rest, unit_cos((4 * col_low + rest) * row_low - turn))
    put(mz_ref, 0, unit_cos(4 * row_low * col_low + turn))
    put(mz_ref, 1, unit_cos(4 * row_low * col_low - turn))


def tables_of(count):
    return (count, 2, HALF, HALF)


def table_call(body, counts, name, operand, spec):
    return pl.pallas_call(
        body,
        in_specs=[spec],
        out_shape=tuple(pltpu.HBM(tables_of(count), bf16) for count in counts),
        out_specs=tuple(RESIDENT for _ in counts),
        compiler_params=params(8),
        name=name,
    )(operand)


def onward_tables(ready):
    return table_call(onward_body, (2, 4), "onward_tables", ready, REMAIN)


def backward_tables(ready):
    return table_call(backward_body, (2, 4, 2), "backward_tables", ready, SCALAR)


TILE = 128
STRIP = 16


def strips(rows, body):
    def step(index, carry):
        body(pl.multiple_of(index * STRIP, STRIP))
        return carry

    lax.fori_loop(0, rows // STRIP, step, 0, unroll=True)


def lane_table(read, count):
    lanes = lax.broadcasted_iota(jnp.int32, (STRIP, LANE), 1)
    table = jnp.zeros((STRIP, LANE), f32)
    for index in range(count):
        table = jnp.where(lanes == index, read(index), table)
    return table


def pick(table, index):
    parts = [
        jnp.take_along_axis(table, index[:, LANE * k : LANE * (k + 1)], axis=1)
        for k in range(N // LANE)
    ]
    return jnp.concatenate(parts, axis=1)


def rows_of(index):
    return pl.ds(pl.multiple_of(index * TILE, TILE), TILE)


def stream(fetch, work, count=N // TILE):
    first = fetch(0)
    for copy in first:
        copy.start()
    for copy in first:
        copy.wait()
    for index in range(1, count):
        for copy in fetch(index):
            copy.start()

    def step(index, carry):
        @pl.when(index > 0)
        def _():
            for copy in fetch(index):
                copy.wait()

        work(index)
        return carry

    lax.fori_loop(0, count, step, 0)


def planes_of(source, target, rows, sems, index, base):
    return tuple(
        pltpu.make_async_copy(source.at[k, rows], target.at[k, rows], sems.at[index, base + k])
        for k in range(COMPS)
    )


def coef_body(
    moduli_hbm, mobility_hbm, rates_hbm, grain_ref, label_ref, strain_ref,
    unit_out, kin_out, dec_out, moduli, mobility, rates, lookup, sems,
):
    grains = mobility.shape[0]

    @pl.when(pl.program_id(0) == 0)
    def _():
        copies = [
            pltpu.make_async_copy(source, target, sems.at[k])
            for k, (source, target) in enumerate(
                ((moduli_hbm, moduli), (mobility_hbm, mobility), (rates_hbm, rates))
            )
        ]
        for copy in copies:
            copy.start()
        for copy in copies:
            copy.wait()
        lookup[0] = lane_table(lambda k: moduli[0, k], grains)
        lookup[1] = lane_table(lambda k: moduli[1, k], grains)
        lookup[2] = lane_table(lambda k: mobility[k], grains)
        lookup[3] = lane_table(lambda k: rates[k - 1] if k else 0.0, rates.shape[0] + 1)

    lames, shears, mobs, speeds = (lookup[k] for k in range(4))

    def strip(start):
        where = pl.ds(start, STRIP)
        grain = grain_ref[where, :]
        lame = pick(lames, grain)
        shear = pick(shears, grain)
        parts = [strain_ref[comp, where, :] for comp in range(COMPS)]
        trace = parts[0] + parts[1] + parts[2]
        square = (
            parts[0] * parts[0]
            + parts[1] * parts[1]
            + parts[2] * parts[2]
            + 2.0 * (parts[3] * parts[3] + parts[4] * parts[4] + parts[5] * parts[5])
        )
        energy = 0.5 * lame * trace * trace + shear * square
        mech = 1.0 + mech_boost * energy / (1.0 + energy)
        kin_out[where, :] = time_step * pick(mobs, grain) * mech
        dec_out[where, :] = time_step * pick(speeds, label_ref[where, :])
        spread = lame * trace
        double = 2.0 * shear
        for comp in range(COMPS):
            part = double * parts[comp]
            unit_out[comp, where, :] = part + spread if comp < 3 else part

    strips(TILE, strip)


PLANE = jax.ShapeDtypeStruct((N, N), f32)
TILES = N // TILE


def coefficients(moduli, mobility, rates, grain, label, strain):
    stripe = pl.BlockSpec((TILE, N), lambda i: (i, 0))
    stack = pl.BlockSpec((COMPS, TILE, N), lambda i: (0, i, 0))
    operands = (moduli, mobility, rates, grain, label, strain)
    return pl.pallas_call(
        coef_body,
        grid=(TILES,),
        in_specs=[REMAIN, REMAIN, REMAIN, stripe, stripe, stack],
        out_specs=[stack, stripe, stripe],
        out_shape=[pltpu.VMEM((COMPS, N, N), f32), pltpu.VMEM((N, N), f32), pltpu.VMEM((N, N), f32)],
        scratch_shapes=[
            pltpu.SMEM(moduli.shape, f32),
            pltpu.SMEM(mobility.shape, f32),
            pltpu.SMEM(rates.shape, f32),
            pltpu.VMEM((4, STRIP, LANE), f32),
            pltpu.SemaphoreType.DMA((3,)),
        ],
        compiler_params=params(16, 1),
        name="coefficients",
    )(*map(in_hbm, operands))


def planar_sum(ref, start):
    center = ref[pl.ds(start, STRIP), :]
    before = ref[pl.ds(pl.multiple_of((start + N - 8) & (N - 1), 8), 8), :]
    after = ref[pl.ds(pl.multiple_of((start + STRIP) & (N - 1), 8), 8), :]
    tall = jnp.concatenate([before, center, after], axis=0)
    height = STRIP + 16
    above = pltpu.roll(tall, 1, 0)[8 : 8 + STRIP]
    below = pltpu.roll(tall, height - 1, 0)[8 : 8 + STRIP]
    sides = pltpu.roll(center, 1, 1) + pltpu.roll(center, N - 1, 1)
    return center, (above + below) + sides


def next_order(p_ref, start, halo_sum, conc_now, kinetic, decay):
    order_now, order_sum = planar_sum(p_ref, start)
    lap_order = order_sum + halo_sum - 6.0 * order_now
    slope = order_now * (1.0 - order_now)
    well_grad = 2.0 * slope * (1.0 - 2.0 * order_now)
    force = (
        grad_coef * lap_order
        - well_height * well_grad
        + drive_coef * 6.0 * slope * (conc_now - conc_eq)
    )
    return order_now + kinetic * force - decay * order_now


def tiles(body):
    def step(index, carry):
        base = pl.multiple_of(index * TILE, TILE)
        strips(TILE, lambda local: body(pl.multiple_of(base + local, STRIP)))
        return carry

    lax.fori_loop(0, N // TILE, step, 0)


def order_body(p_ref, c_ref, up_ref, down_ref, kin_ref, dec_ref, p_out):
    def strip(start):
        where = pl.ds(start, STRIP)
        p_out[where, :] = next_order(
            p_ref,
            start,
            up_ref[where, :] + down_ref[where, :],
            c_ref[where, :],
            kin_ref[where, :],
            dec_ref[where, :],
        )

    tiles(strip)


def order_step(order_now, conc_now, halos, kinetic, decay):
    planes = (order_now, conc_now, *halos, kinetic, decay)
    return pl.pallas_call(
        order_body,
        in_specs=[RESIDENT] * 6,
        out_specs=RESIDENT,
        out_shape=PLANE,
        compiler_params=params(8),
        name="order_step",
    )(*planes)


def next_conc(c_ref, start, halo_sum, order_now, order_new):
    conc_now, conc_sum = planar_sum(c_ref, start)
    lap_conc = conc_sum + halo_sum - 6.0 * conc_now
    return (
        conc_now + time_step * diffusivity * lap_conc + release_coef * (order_now - order_new)
    )


def conc_body(c_ref, p_ref, new_ref, up_ref, down_ref, *refs):
    c_out = refs[-1]

    def strip(start):
        where = pl.ds(start, STRIP)
        halo_sum = up_ref[where, :] + down_ref[where, :]
        c_out[where, :] = next_conc(c_ref, start, halo_sum, p_ref[where, :], new_ref[where, :])

    tiles(strip)


def conc_step(conc_now, order_now, order_new, halos, after=()):
    planes = (conc_now, order_now, order_new, *halos)
    return pl.pallas_call(
        conc_body,
        in_specs=[RESIDENT] * 5 + [REMAIN] * len(after),
        out_specs=RESIDENT,
        out_shape=PLANE,
        compiler_params=params(8),
        name="conc_step",
    )(*planes, *map(in_hbm, after))


def butterflies(spectra, comp, lanes_r, lanes_i, odd):
    reals = [spectra[comp, pl.ds(LANE * j, LANE), lanes_r] for j in range(RADIX)]
    imags = [spectra[comp, pl.ds(LANE * j, LANE), lanes_i] for j in range(RADIX)]
    if odd:
        er, ei = reals[0] - reals[2], imags[0] - imags[2]
        turned_r, turned_i = imags[1] - imags[3], reals[3] - reals[1]
    else:
        er, ei = reals[0] + reals[2], imags[0] + imags[2]
        turned_r, turned_i = reals[1] + reals[3], imags[1] + imags[3]
    return (er + turned_r, ei + turned_i), (er - turned_r, ei - turned_i)


def forward_body(
    p_ref, c_ref, up_hbm, down_hbm, kin_hbm, dec_hbm, unit_hbm, txf_hbm, mq_hbm,
    out_ref, p_hbm, up_ref, down_ref, kin_ref, dec_ref, unit_ref, txf_ref, mq_ref, p_out, spectra, packed, highs, lows,
    in_sems, table_sems, order_sems, sems,
):
    def fetch(index):
        rows = rows_of(index)
        singles = (
            (up_hbm, up_ref),
            (down_hbm, down_ref),
            (kin_hbm, kin_ref),
            (dec_hbm, dec_ref),
        )
        return (
            *(
                pltpu.make_async_copy(source.at[rows], target.at[rows], in_sems.at[index, COMPS + k])
                for k, (source, target) in enumerate(singles)
            ),
            *planes_of(unit_hbm, unit_ref, rows, in_sems, index, 0),
        )

    def keep(index):
        rows = rows_of(index)
        return pltpu.make_async_copy(p_out.at[rows], p_hbm.at[rows], order_sems.at[index])

    txf_copy = pltpu.make_async_copy(txf_hbm, txf_ref, table_sems.at[0])
    mq_copy = pltpu.make_async_copy(mq_hbm, mq_ref, table_sems.at[1])
    txf_copy.start()

    def tile(index):
        base = pl.multiple_of(index * TILE, TILE)

        def strip(local):
            start = pl.multiple_of(base + local, STRIP)
            where = pl.ds(start, STRIP)
            order = next_order(
                p_ref,
                start,
                up_ref[where, :] + down_ref[where, :],
                c_ref[where, :],
                kin_ref[where, :],
                dec_ref[where, :],
            )
            p_out[where, :] = order
            scale = order * order * (3.0 - 2.0 * order) + residual_stiff
            for comp in range(COMPS):
                part = scale * unit_ref[comp, where, :]
                left = part[:, :HALF]
                right = part[:, HALF:]
                here = pl.ds(pl.multiple_of(comp * TILE + local, STRIP), STRIP)
                for parity, folded in ((0, left + right), (1, left - right)):
                    highs[parity, here, :], lows[parity, here, :] = split(folded)

        strips(TILE, strip)
        keep(index).start()

        @pl.when(index == 0)
        def _():
            mq_copy.start()
            txf_copy.wait()

        for parity in range(2):
            high = highs[parity]
            result = (
                mul(high, txf_ref[parity, 0])
                + mul(lows[parity], txf_ref[parity, 0])
                + mul(high, txf_ref[parity, 1])
            )
            for comp in range(COMPS):
                spectra[comp, pl.ds(base, TILE), pl.ds(HALF * parity, HALF)] = result[
                    comp * TILE : (comp + 1) * TILE
                ]

    stream(fetch, tile)
    mq_copy.wait()

    flat = packed.reshape(LANE * PITCH, LANE)
    copies = []
    for odd in range(2):
        for pair in range(PAIRS):
            for parity in range(2):
                lanes_r = pl.ds(HALF * parity, LANE)
                lanes_i = pl.ds(HALF * parity + LANE, LANE)
                both = [butterflies(spectra, 2 * pair + k, lanes_r, lanes_i, odd) for k in (0, 1)]
                for half in range(2):
                    rest = odd + 2 * half
                    real = jnp.concatenate([both[0][half][0], both[1][half][0]], axis=1)
                    imag = jnp.concatenate([both[0][half][1], both[1][half][1]], axis=1)
                    value = jnp.concatenate([real, imag], axis=0)
                    result = table_times((mq_ref[rest, 0], mq_ref[rest, 1]), value)
                    give_pair(flat, (pair * RADIX + rest) * SUB + parity * 4, result)
            for rest in (odd, odd + 2):
                block = pair * RADIX + rest
                copy = pltpu.make_async_copy(packed.at[:, block], out_ref.at[:, block], sems.at[block])
                copy.start()
                copies.append(copy)
    for copy in copies:
        copy.wait()
    for index in range(N // TILE):
        keep(index).wait()


def give_pair(flat, row, result):
    for k in (0, 1):
        lanes = slice(LANE * k, LANE * (k + 1))
        flat[pl.ds(row + 2 * k, LANE, stride=PITCH), :] = result[:LANE, lanes]
        flat[pl.ds(row + 2 * k + 1, LANE, stride=PITCH), :] = result[LANE:, lanes]


def take_pair(flat, row):
    reals, imags = [], []
    for k in (0, 1):
        reals.append(flat[pl.ds(row + 2 * k, LANE, stride=PITCH), :])
        imags.append(flat[pl.ds(row + 2 * k + 1, LANE, stride=PITCH), :])
    return jnp.concatenate(
        [jnp.concatenate(reals, axis=1), jnp.concatenate(imags, axis=1)], axis=0
    )


SHAPE = (LANE, BLOCKS, SUB, LANE)
SPACED = (LANE, BLOCKS + 1, SUB, LANE)
BUFFER = pltpu.HBM(SHAPE, f32)


def forward(order, conc, halos, kinetic, decay, unit, txf, mq):
    return pl.pallas_call(
        forward_body,
        in_specs=[RESIDENT] * 2 + [REMAIN] * 7,
        out_specs=(REMAIN, REMAIN),
        out_shape=(BUFFER, pltpu.HBM((N, N), f32)),
        scratch_shapes=[
            *[pltpu.VMEM((N, N), f32)] * 4,
            pltpu.VMEM((COMPS, N, N), f32),
            pltpu.VMEM(tables_of(2), bf16),
            pltpu.VMEM(tables_of(4), bf16),
            pltpu.VMEM((N, N), f32),
            pltpu.VMEM((COMPS, N, N), f32),
            pltpu.VMEM(SPACED, f32),
            pltpu.VMEM((2, COMPS * TILE, HALF), bf16),
            pltpu.VMEM((2, COMPS * TILE, HALF), bf16),
            pltpu.SemaphoreType.DMA((N // TILE, COMPS + 4)),
            pltpu.SemaphoreType.DMA((2,)),
            pltpu.SemaphoreType.DMA((N // TILE,)),
            pltpu.SemaphoreType.DMA((BLOCKS,)),
        ],
        compiler_params=params(40),
        name="forward",
    )(order, conc, *map(in_hbm, (*halos, kinetic, decay, unit, txf, mq)))


def middle_body(
    band_ref, in_ref, mz_hbm, out_ref, received, mz_ref, packed, in_sems, out_sems, table_sem
):
    source = received.reshape(LANE * PITCH, LANE)
    flat = packed.reshape(LANE * PITCH, LANE)

    def fetch(pair, rest):
        block = pair * RADIX + rest
        return pltpu.make_async_copy(in_ref.at[:, block], received.at[:, block], in_sems.at[block])

    def send(pair, rest):
        block = pair * RADIX + rest
        return pltpu.make_async_copy(packed.at[:, block], out_ref.at[:, block], out_sems.at[block])

    mz_copy = pltpu.make_async_copy(mz_hbm, mz_ref, table_sem)
    for pair in range(PAIRS):
        fetch(pair, 0).start()
    mz_copy.start()
    for pair in range(PAIRS):
        fetch(pair, 0).wait()
    for rest in range(1, RADIX):
        for pair in range(PAIRS):
            fetch(pair, rest).start()
    mz_copy.wait()

    def step(rest, carry):
        @pl.when(rest > 0)
        def _():
            for pair in range(PAIRS):
                fetch(pair, rest).wait()

        middle_step(band_ref, source, mz_ref, flat, rest)
        for pair in range(PAIRS):
            send(pair, rest).start()
        return carry

    lax.fori_loop(0, RADIX, step, 0)
    for rest in range(RADIX):
        for pair in range(PAIRS):
            send(pair, rest).wait()


def middle_step(band_ref, source, mz_ref, flat, rest):
    onward = (mz_ref[0, 0], mz_ref[0, 1])
    backward = (mz_ref[1, 0], mz_ref[1, 1])
    shape = (DEPTH, LANE)
    depth_index = lax.broadcasted_iota(jnp.int32, shape, 0)
    xi_z = jnp.where(depth_index < DEPTH // 2, depth_index, depth_index - DEPTH).astype(f32)
    wave_y = band_ref[0] * RADIX + rest
    xi_y = jnp.where(wave_y < N // 2, wave_y, wave_y - N).astype(f32)
    for parity in range(2):
        tau_r, tau_i = [], []
        for pair in range(PAIRS):
            result = table_times(onward, take_pair(source, (pair * RADIX + rest) * SUB + parity * 4))
            for k in (0, 1):
                lanes = slice(LANE * k, LANE * (k + 1))
                tau_r.append(result[:LANE, lanes])
                tau_i.append(result[LANE:, lanes])
        xi_x = (2 * lax.broadcasted_iota(jnp.int32, shape, 1) + parity).astype(f32)
        wave_sq = xi_x * xi_x + xi_y * xi_y + xi_z * xi_z
        live = (wave_sq > 0.5) & (xi_x < float(HALF))
        safe = jnp.where(live, wave_sq, 1.0)
        inverse = 1.0 / safe
        first = jnp.where(live, (0.5 / shear_ref) * inverse, 0.0)
        second = jnp.where(live, (0.5 * coupling) * (inverse * inverse), 0.0)
        grids = []
        for tau in (tau_r, tau_i):
            t_xx, t_yy, t_zz, t_yz, t_xz, t_xy = tau
            v_x = t_xx * xi_x + t_xy * xi_y + t_xz * xi_z
            v_y = t_xy * xi_x + t_yy * xi_y + t_yz * xi_z
            v_z = t_xz * xi_x + t_yz * xi_y + t_zz * xi_z
            inner = (xi_x * v_x + xi_y * v_y + xi_z * v_z) * second
            h_x = v_x * first - xi_x * inner
            h_y = v_y * first - xi_y * inner
            h_z = v_z * first - xi_z * inner
            grids.append(
                (
                    2.0 * xi_x * h_x,
                    2.0 * xi_y * h_y,
                    2.0 * xi_z * h_z,
                    xi_z * h_y + xi_y * h_z,
                    xi_z * h_x + xi_x * h_z,
                    xi_y * h_x + xi_x * h_y,
                )
            )
        for pair in range(PAIRS):
            real = jnp.concatenate([grids[0][pair * 2], grids[0][pair * 2 + 1]], axis=1)
            imag = jnp.concatenate([grids[1][pair * 2], grids[1][pair * 2 + 1]], axis=1)
            result = table_times(backward, jnp.concatenate([real, imag], axis=0))
            give_pair(flat, (pair * RADIX + rest) * SUB + parity * 4, result)


def middle(band, received, mz):
    return pl.pallas_call(
        middle_body,
        in_specs=[SCALAR, REMAIN, REMAIN],
        out_specs=REMAIN,
        out_shape=BUFFER,
        scratch_shapes=[
            pltpu.VMEM(SPACED, f32),
            pltpu.VMEM(tables_of(2), bf16),
            pltpu.VMEM(SPACED, f32),
            pltpu.SemaphoreType.DMA((BLOCKS,)),
            pltpu.SemaphoreType.DMA((BLOCKS,)),
            pltpu.SemaphoreType.DMA(()),
        ],
        compiler_params=params(24),
        name="middle",
    )(band, in_hbm(received), in_hbm(mz))


def inverse_y(source, mqi_ref, pair, parity):
    blocks = []
    for rest in range(RADIX):
        value = take_pair(source, (pair * RADIX + rest) * SUB + parity * 4)
        result = table_times((mqi_ref[rest, 0], mqi_ref[rest, 1]), value)
        blocks.append((result[:LANE], result[LANE:]))
    er0, er1 = blocks[0][0] + blocks[2][0], blocks[0][0] - blocks[2][0]
    ei0, ei1 = blocks[0][1] + blocks[2][1], blocks[0][1] - blocks[2][1]
    or0, or1 = blocks[1][0] + blocks[3][0], blocks[1][0] - blocks[3][0]
    oi0, oi1 = blocks[1][1] + blocks[3][1], blocks[1][1] - blocks[3][1]
    return (
        (er0 + or0, ei0 + oi0),
        (er1 - oi1, ei1 + or1),
        (er0 - or0, ei0 - oi0),
        (er1 + oi1, ei1 - or1),
    )


def inverse_body(
    in_ref, strain_hbm, mqi_hbm, txi_hbm, out_ref, received, strain_ref, mqi_ref, txi_ref, moved,
    in_sems, strain_sems, table_sems, sems,
):
    source = received.reshape(LANE * PITCH, LANE)

    def fetch(pair, rest):
        block = pair * RADIX + rest
        return pltpu.make_async_copy(in_ref.at[:, block], received.at[:, block], in_sems.at[block])

    def fetch_strain(comp):
        return pltpu.make_async_copy(strain_hbm.at[comp], strain_ref.at[comp], strain_sems.at[comp])

    mqi_copy = pltpu.make_async_copy(mqi_hbm, mqi_ref, table_sems.at[0])
    txi_copy = pltpu.make_async_copy(txi_hbm, txi_ref, table_sems.at[1])
    def copy_of(comp):
        return pltpu.make_async_copy(moved.at[comp], out_ref.at[comp], sems.at[comp])

    for rest in range(RADIX):
        fetch(0, rest).start()
    mqi_copy.start()
    txi_copy.start()
    for rest in range(RADIX):
        fetch(0, rest).wait()
    mqi_copy.wait()
    txi_copy.wait()
    for pair in range(PAIRS):
        for k in (0, 1):
            fetch_strain(2 * pair + k).start()
        if pair + 1 < PAIRS:
            for rest in range(RADIX):
                fetch(pair + 1, rest).start()

    def step(pair, carry):
        @pl.when(pair > 0)
        def _():
            for rest in range(RADIX):
                fetch(pair, rest).wait()

        planes = [inverse_y(source, mqi_ref, pair, parity) for parity in range(2)]
        for k in (0, 1):
            fetch_strain(2 * pair + k).wait()
        for k in (0, 1):
            comp = pair * 2 + k
            lanes = slice(LANE * k, LANE * (k + 1))
            halves = []
            for parity in range(2):
                value = jnp.concatenate(
                    [
                        jnp.concatenate([real[:, lanes], imag[:, lanes]], axis=1)
                        for real, imag in planes[parity]
                    ],
                    axis=0,
                )
                halves.append(times_table(value, (txi_ref[parity, 0], txi_ref[parity, 1])))
            even, odd = halves
            left = pl.ds(0, HALF)
            right = pl.ds(HALF, HALF)
            moved[comp, :, left] = strain_ref[comp, :, left] - (even + odd)
            moved[comp, :, right] = strain_ref[comp, :, right] - (even - odd)
            copy_of(comp).start()
        return carry

    lax.fori_loop(0, PAIRS, step, 0)
    for comp in range(COMPS):
        copy_of(comp).wait()


def inverse(returned, strain, mqi, txi):
    return pl.pallas_call(
        inverse_body,
        in_specs=[REMAIN] * 4,
        out_specs=REMAIN,
        out_shape=pltpu.HBM((COMPS, N, N), f32),
        scratch_shapes=[
            pltpu.VMEM(SPACED, f32),
            pltpu.VMEM((COMPS, N, N), f32),
            pltpu.VMEM(tables_of(4), bf16),
            pltpu.VMEM(tables_of(2), bf16),
            pltpu.VMEM((COMPS, N, N), f32),
            pltpu.SemaphoreType.DMA((BLOCKS,)),
            pltpu.SemaphoreType.DMA((COMPS,)),
            pltpu.SemaphoreType.DMA((2,)),
            pltpu.SemaphoreType.DMA((COMPS,)),
        ],
        compiler_params=params(32),
        name="inverse",
    )(in_hbm(returned), in_hbm(strain), in_hbm(mqi), in_hbm(txi))


def exchange(block):
    packed = block.reshape(DEPTH, ROWS, LANE)
    moved = lax.all_to_all(packed, "gz", split_axis=0, concat_axis=0, tiled=True)
    return moved.reshape(SHAPE)


def neighbours(plane, count):
    ahead = [(i, (i + 1) % count) for i in range(count)]
    behind = [((i + 1) % count, i) for i in range(count)]
    return lax.ppermute(plane, "gz", ahead), lax.ppermute(plane, "gz", behind)


def shards(
    order_param,
    concentration,
    strain,
    grain_ids,
    seed_labels,
    grain_moduli,
    grain_mobility,
    seed_rate,
):
    count = lax.axis_size("gz")
    order_now = order_param.reshape(N, N)
    conc_now = concentration.reshape(N, N)
    planes = strain.reshape(COMPS, N, N)
    order_halos = neighbours(order_now, count)
    conc_halos = neighbours(conc_now, count)
    unit, kinetic, decay = coefficients(
        grain_moduli,
        grain_mobility,
        seed_rate,
        grain_ids.reshape(N, N),
        seed_labels.reshape(N, N),
        planes,
    )
    for _ in range(SUBSTEPS - 1):
        order_new = order_step(order_now, conc_now, order_halos, kinetic, decay)
        order_halos = neighbours(order_new, count)
        txf, mq = onward_tables(conc_halos[0])
        conc_new = conc_step(conc_now, order_now, order_new, conc_halos, (txf,))
        conc_halos = neighbours(conc_new, count)
        order_now, conc_now = order_new, conc_new
    spectra, order_next = forward(
        order_now, conc_now, order_halos, kinetic, decay, unit, txf, mq
    )
    band = lax.axis_index("gz").astype(jnp.int32).reshape(1)
    spectra, band, conc_halos = lax.optimization_barrier((spectra, band, conc_halos))
    received = exchange(spectra)
    mz, mqi, txi = backward_tables(band)
    conc_next = conc_step(conc_now, order_now, order_next, conc_halos)
    returned = exchange(middle(band, received, mz))
    strain_next = inverse(returned, planes, mqi, txi)
    return (
        order_next.reshape(1, N, N),
        conc_next.reshape(1, N, N),
        strain_next.reshape(COMPS, 1, N, N),
    )


def solution(mesh):
    return jax.shard_map(
        shards,
        mesh=mesh,
        in_specs=(
            P("gz", None, None),
            P("gz", None, None),
            P(None, "gz", None, None),
            P("gz", None, None),
            P("gz", None, None),
            P(),
            P(),
            P(),
        ),
        out_specs=(P("gz", None, None), P("gz", None, None), P(None, "gz", None, None)),
        check_vma=False,
    )
```

```python
import functools
import math

import jax
import jax.numpy as jnp
from jax import lax
from jax.experimental import pallas as pl
from jax.experimental.pallas import tpu as pltpu
from jax.sharding import PartitionSpec as P

SUBSTEPS = 2
N = 512
HALF = 256
LANE = 128
DEPTH = 128
COMPS = 6
RADIX = 4
FIELDS = 5
SUB = 8
BLOCKS = 2 * FIELDS
ROWS = BLOCKS * SUB
PITCH = (BLOCKS + 1) * SUB

time_step = 0.05
grad_coef = 1.0
well_height = 1.0
drive_coef = 2.0
conc_eq = 0.5
mech_boost = 1.0
diffusivity = 1.0
release_coef = 1.0
residual_stiff = 0.1
lame_ref = 1.0
shear_ref = 1.0
coupling = (lame_ref + shear_ref) / (shear_ref * (lame_ref + 2.0 * shear_ref))

f32 = jnp.float32
bf16 = jnp.bfloat16
MIB = 1024 * 1024


def params(mib, dims=0):
    semantics = ("arbitrary",) * dims if dims else None
    return pltpu.CompilerParams(dimension_semantics=semantics, vmem_limit_bytes=mib * MIB)


def in_hbm(value):
    return pltpu.with_memory_space_constraint(value, pltpu.HBM)


RESIDENT = pl.BlockSpec(memory_space=pltpu.VMEM)
REMAIN = pl.BlockSpec(memory_space=pl.ANY)
SCALAR = pl.BlockSpec(memory_space=pltpu.SMEM)


def split(value):
    high = value.astype(bf16)
    low = (value - high.astype(f32)).astype(bf16)
    return high, low


def mul(left, right):
    return lax.dot_general(
        left, right, (((1,), (0,)), ((), ())), preferred_element_type=f32
    )


def table_times(table, value):
    high, low = split(value)
    return mul(table[0], high) + mul(table[0], low) + mul(table[1], high)


def times_table(value, table):
    high, low = split(value)
    return mul(high, table[0]) + mul(low, table[0]) + mul(high, table[1])


def unit_cos(index):
    wrapped = ((index + 256) & 511) - 256
    angle = (128 - jnp.abs(wrapped)).astype(f32) * (2.0 * math.pi / 512.0)
    square = angle * angle
    poly = 1.0 / 6227020800.0
    for power in (39916800.0, 362880.0, 5040.0, 120.0, 6.0):
        poly = 1.0 / power - square * poly
    return angle * (1.0 - square * poly)


def table_grid():
    rows = lax.broadcasted_iota(jnp.int32, (HALF, HALF), 0)
    cols = lax.broadcasted_iota(jnp.int32, (HALF, HALF), 1)
    turn = ((rows >> 7) - (cols >> 7)) * 128
    return rows, cols, rows & 127, cols & 127, turn


def put(ref, slot, value):
    high, low = split(value)
    ref[slot, 0] = high
    ref[slot, 1] = low


def onward_body(order_ref, txf_ref, mq_ref):
    rows, cols, row_low, col_low, turn = table_grid()
    for parity in range(2):
        wave = 2 * col_low + parity
        put(txf_ref, parity, unit_cos(rows * wave + (cols >> 7) * 128))
    for rest in range(RADIX):
        put(mq_ref, rest, unit_cos((4 * row_low + rest) * col_low + turn))


def backward_body(order_ref, mz_ref, mqi_ref, txi_ref):
    rows, cols, row_low, col_low, turn = table_grid()
    for parity in range(2):
        wave = 2 * row_low + parity
        weight = jnp.where(wave == 0, 1.0, 2.0) * (1.0 / float(N * N * DEPTH))
        put(txi_ref, parity, unit_cos(wave * cols + (rows >> 7) * 128) * weight)
    for rest in range(RADIX):
        put(mqi_ref, rest, unit_cos((4 * col_low + rest) * row_low - turn))
    put(mz_ref, 0, unit_cos(4 * row_low * col_low + turn))
    put(mz_ref, 1, unit_cos(4 * row_low * col_low - turn))


def tables_of(count):
    return (count, 2, HALF, HALF)


def table_call(body, counts, name, operand, spec):
    return pl.pallas_call(
        body,
        in_specs=[spec],
        out_shape=tuple(pltpu.HBM(tables_of(count), bf16) for count in counts),
        out_specs=tuple(RESIDENT for _ in counts),
        compiler_params=params(8),
        name=name,
    )(operand)


def onward_tables(ready):
    return table_call(onward_body, (2, 4), "onward_tables", ready, REMAIN)


def backward_tables(ready):
    return table_call(backward_body, (2, 4, 2), "backward_tables", ready, SCALAR)


TILE = 128
STRIP = 16


def strips(rows, body):
    def step(index, carry):
        body(pl.multiple_of(index * STRIP, STRIP))
        return carry

    lax.fori_loop(0, rows // STRIP, step, 0, unroll=True)


def lane_table(read, count):
    lanes = lax.broadcasted_iota(jnp.int32, (STRIP, LANE), 1)
    table = jnp.zeros((STRIP, LANE), f32)
    for index in range(count):
        table = jnp.where(lanes == index, read(index), table)
    return table


def pick(table, index):
    parts = [
        jnp.take_along_axis(table, index[:, LANE * k : LANE * (k + 1)], axis=1)
        for k in range(N // LANE)
    ]
    return jnp.concatenate(parts, axis=1)


def rows_of(index):
    return pl.ds(pl.multiple_of(index * TILE, TILE), TILE)


def stream(fetch, work, count=N // TILE):
    first = fetch(0)
    for copy in first:
        copy.start()
    for copy in first:
        copy.wait()
    for index in range(1, count):
        for copy in fetch(index):
            copy.start()

    def step(index, carry):
        @pl.when(index > 0)
        def _():
            for copy in fetch(index):
                copy.wait()

        work(index)
        return carry

    lax.fori_loop(0, count, step, 0)


def planes_of(source, target, rows, sems, index, base):
    return tuple(
        pltpu.make_async_copy(source.at[k, rows], target.at[k, rows], sems.at[index, base + k])
        for k in range(COMPS)
    )


def coef_body(
    moduli_hbm, mobility_hbm, rates_hbm, grain_ref, label_ref, strain_ref,
    unit_out, kin_out, dec_out, moduli, mobility, rates, lookup, sems,
):
    grains = mobility.shape[0]

    @pl.when(pl.program_id(0) == 0)
    def _():
        copies = [
            pltpu.make_async_copy(source, target, sems.at[k])
            for k, (source, target) in enumerate(
                ((moduli_hbm, moduli), (mobility_hbm, mobility), (rates_hbm, rates))
            )
        ]
        for copy in copies:
            copy.start()
        for copy in copies:
            copy.wait()
        lookup[0] = lane_table(lambda k: moduli[0, k], grains)
        lookup[1] = lane_table(lambda k: moduli[1, k], grains)
        lookup[2] = lane_table(lambda k: mobility[k], grains)
        lookup[3] = lane_table(lambda k: rates[k - 1] if k else 0.0, rates.shape[0] + 1)

    lames, shears, mobs, speeds = (lookup[k] for k in range(4))

    def strip(start):
        where = pl.ds(start, STRIP)
        grain = grain_ref[where, :]
        lame = pick(lames, grain)
        shear = pick(shears, grain)
        parts = [strain_ref[comp, where, :] for comp in range(COMPS)]
        trace = parts[0] + parts[1] + parts[2]
        square = (
            parts[0] * parts[0]
            + parts[1] * parts[1]
            + parts[2] * parts[2]
            + 2.0 * (parts[3] * parts[3] + parts[4] * parts[4] + parts[5] * parts[5])
        )
        energy = 0.5 * lame * trace * trace + shear * square
        mech = 1.0 + mech_boost * energy / (1.0 + energy)
        kin_out[where, :] = time_step * pick(mobs, grain) * mech
        dec_out[where, :] = time_step * pick(speeds, label_ref[where, :])
        spread = lame * trace
        double = 2.0 * shear
        for comp in range(COMPS):
            part = double * parts[comp]
            unit_out[comp, where, :] = part + spread if comp < 3 else part

    strips(TILE, strip)


PLANE = jax.ShapeDtypeStruct((N, N), f32)
TILES = N // TILE


def coefficients(moduli, mobility, rates, grain, label, strain):
    stripe = pl.BlockSpec((TILE, N), lambda i: (i, 0))
    stack = pl.BlockSpec((COMPS, TILE, N), lambda i: (0, i, 0))
    operands = (moduli, mobility, rates, grain, label, strain)
    return pl.pallas_call(
        coef_body,
        grid=(TILES,),
        in_specs=[REMAIN, REMAIN, REMAIN, stripe, stripe, stack],
        out_specs=[stack, stripe, stripe],
        out_shape=[pltpu.VMEM((COMPS, N, N), f32), pltpu.VMEM((N, N), f32), pltpu.VMEM((N, N), f32)],
        scratch_shapes=[
            pltpu.SMEM(moduli.shape, f32),
            pltpu.SMEM(mobility.shape, f32),
            pltpu.SMEM(rates.shape, f32),
            pltpu.VMEM((4, STRIP, LANE), f32),
            pltpu.SemaphoreType.DMA((3,)),
        ],
        compiler_params=params(16, 1),
        name="coefficients",
    )(*map(in_hbm, operands))


def planar_sum(ref, start):
    center = ref[pl.ds(start, STRIP), :]
    before = ref[pl.ds(pl.multiple_of((start + N - 8) & (N - 1), 8), 8), :]
    after = ref[pl.ds(pl.multiple_of((start + STRIP) & (N - 1), 8), 8), :]
    tall = jnp.concatenate([before, center, after], axis=0)
    height = STRIP + 16
    above = pltpu.roll(tall, 1, 0)[8 : 8 + STRIP]
    below = pltpu.roll(tall, height - 1, 0)[8 : 8 + STRIP]
    sides = pltpu.roll(center, 1, 1) + pltpu.roll(center, N - 1, 1)
    return center, (above + below) + sides


def next_order(p_ref, start, halo_sum, conc_now, kinetic, decay):
    order_now, order_sum = planar_sum(p_ref, start)
    lap_order = order_sum + halo_sum - 6.0 * order_now
    slope = order_now * (1.0 - order_now)
    well_grad = 2.0 * slope * (1.0 - 2.0 * order_now)
    force = (
        grad_coef * lap_order
        - well_height * well_grad
        + drive_coef * 6.0 * slope * (conc_now - conc_eq)
    )
    return order_now + kinetic * force - decay * order_now


def tiles(body):
    def step(index, carry):
        base = pl.multiple_of(index * TILE, TILE)
        strips(TILE, lambda local: body(pl.multiple_of(base + local, STRIP)))
        return carry

    lax.fori_loop(0, N // TILE, step, 0)


def order_body(p_ref, c_ref, up_ref, down_ref, kin_ref, dec_ref, p_out):
    def strip(start):
        where = pl.ds(start, STRIP)
        p_out[where, :] = next_order(
            p_ref,
            start,
            up_ref[where, :] + down_ref[where, :],
            c_ref[where, :],
            kin_ref[where, :],
            dec_ref[where, :],
        )

    tiles(strip)


def order_step(order_now, conc_now, halos, kinetic, decay):
    planes = (order_now, conc_now, *halos, kinetic, decay)
    return pl.pallas_call(
        order_body,
        in_specs=[RESIDENT] * 6,
        out_specs=RESIDENT,
        out_shape=PLANE,
        compiler_params=params(8),
        name="order_step",
    )(*planes)


def next_conc(c_ref, start, halo_sum, order_now, order_new):
    conc_now, conc_sum = planar_sum(c_ref, start)
    lap_conc = conc_sum + halo_sum - 6.0 * conc_now
    return (
        conc_now + time_step * diffusivity * lap_conc + release_coef * (order_now - order_new)
    )


def conc_body(c_ref, p_ref, new_ref, up_ref, down_ref, *refs):
    c_out = refs[-1]

    def strip(start):
        where = pl.ds(start, STRIP)
        halo_sum = up_ref[where, :] + down_ref[where, :]
        c_out[where, :] = next_conc(c_ref, start, halo_sum, p_ref[where, :], new_ref[where, :])

    tiles(strip)


def conc_step(conc_now, order_now, order_new, halos, after=()):
    planes = (conc_now, order_now, order_new, *halos)
    return pl.pallas_call(
        conc_body,
        in_specs=[RESIDENT] * 5 + [REMAIN] * len(after),
        out_specs=RESIDENT,
        out_shape=PLANE,
        compiler_params=params(8),
        name="conc_step",
    )(*planes, *map(in_hbm, after))


def waves_x(rows):
    lanes = lax.broadcasted_iota(jnp.int32, (rows, HALF), 1)
    return (2 * (lanes & (LANE - 1)) + (lanes >> 7)).astype(f32)


def waves_y(rows, rest):
    index = RADIX * (lax.broadcasted_iota(jnp.int32, (rows, HALF), 0) & (LANE - 1)) + rest
    return jnp.where(index < N // 2, index, index - N).astype(f32)


def give(flat, block, half, value):
    row = block * SUB + half * 4
    for parity in range(2):
        lanes = slice(LANE * parity, LANE * (parity + 1))
        flat[pl.ds(row + 2 * parity, LANE, stride=PITCH), :] = value[:LANE, lanes]
        flat[pl.ds(row + 2 * parity + 1, LANE, stride=PITCH), :] = value[LANE:, lanes]


def take(flat, block, half):
    row = block * SUB + half * 4
    parts = [
        jnp.concatenate(
            [flat[pl.ds(row + 2 * parity + k, LANE, stride=PITCH), :] for parity in range(2)],
            axis=1,
        )
        for k in range(2)
    ]
    return jnp.concatenate(parts, axis=0)


def both_parities(spectra, comp, j, shift):
    rows = pl.ds(LANE * j, LANE)
    return jnp.concatenate(
        [spectra[comp, rows, pl.ds(HALF * parity + shift, LANE)] for parity in range(2)], axis=1
    )


def butterflies(spectra, comp, odd):
    reals = [both_parities(spectra, comp, j, 0) for j in range(RADIX)]
    imags = [both_parities(spectra, comp, j, LANE) for j in range(RADIX)]
    if odd:
        er, ei = reals[0] - reals[2], imags[0] - imags[2]
        turned_r, turned_i = imags[1] - imags[3], reals[3] - reals[1]
    else:
        er, ei = reals[0] + reals[2], imags[0] + imags[2]
        turned_r, turned_i = reals[1] + reals[3], imags[1] + imags[3]
    return (
        jnp.concatenate([er + turned_r, ei + turned_i], axis=0),
        jnp.concatenate([er - turned_r, ei - turned_i], axis=0),
    )


def forward_body(
    p_ref, c_ref, up_hbm, down_hbm, kin_hbm, dec_hbm, unit_hbm, txf_hbm, mq_hbm,
    out_ref, p_hbm, up_ref, down_ref, kin_ref, dec_ref, unit_ref, txf_ref, mq_ref, p_out, spectra, packed, highs, lows,
    in_sems, table_sems, order_sems, sems,
):
    def fetch(index):
        rows = rows_of(index)
        singles = (
            (up_hbm, up_ref),
            (down_hbm, down_ref),
            (kin_hbm, kin_ref),
            (dec_hbm, dec_ref),
        )
        return (
            *(
                pltpu.make_async_copy(source.at[rows], target.at[rows], in_sems.at[index, COMPS + k])
                for k, (source, target) in enumerate(singles)
            ),
            *planes_of(unit_hbm, unit_ref, rows, in_sems, index, 0),
        )

    def keep(index):
        rows = rows_of(index)
        return pltpu.make_async_copy(p_out.at[rows], p_hbm.at[rows], order_sems.at[index])

    txf_copy = pltpu.make_async_copy(txf_hbm, txf_ref, table_sems.at[0])
    mq_copy = pltpu.make_async_copy(mq_hbm, mq_ref, table_sems.at[1])
    txf_copy.start()

    def tile(index):
        base = pl.multiple_of(index * TILE, TILE)

        def strip(local):
            start = pl.multiple_of(base + local, STRIP)
            where = pl.ds(start, STRIP)
            order = next_order(
                p_ref,
                start,
                up_ref[where, :] + down_ref[where, :],
                c_ref[where, :],
                kin_ref[where, :],
                dec_ref[where, :],
            )
            p_out[where, :] = order
            scale = order * order * (3.0 - 2.0 * order) + residual_stiff
            for comp in range(COMPS):
                part = scale * unit_ref[comp, where, :]
                left = part[:, :HALF]
                right = part[:, HALF:]
                here = pl.ds(pl.multiple_of(comp * TILE + local, STRIP), STRIP)
                for parity, folded in ((0, left + right), (1, left - right)):
                    highs[parity, here, :], lows[parity, here, :] = split(folded)

        strips(TILE, strip)
        keep(index).start()

        @pl.when(index == 0)
        def _():
            mq_copy.start()
            txf_copy.wait()

        for parity in range(2):
            high = highs[parity]
            result = (
                mul(high, txf_ref[parity, 0])
                + mul(lows[parity], txf_ref[parity, 0])
                + mul(high, txf_ref[parity, 1])
            )
            for comp in range(COMPS):
                spectra[comp, pl.ds(base, TILE), pl.ds(HALF * parity, HALF)] = result[
                    comp * TILE : (comp + 1) * TILE
                ]

    stream(fetch, tile)
    mq_copy.wait()

    flat = packed.reshape(LANE * PITCH, LANE)
    copies = []

    def send(block):
        copy = pltpu.make_async_copy(packed.at[:, block], out_ref.at[:, block], sems.at[block])
        copy.start()
        copies.append(copy)

    xi_x = waves_x(HALF)
    for odd in range(2):

        def spectrum(comp):
            return [
                table_times((mq_ref[odd + 2 * half, 0], mq_ref[odd + 2 * half, 1]), value)
                for half, value in enumerate(butterflies(spectra, comp, odd))
            ]

        for field, comp in ((2, 4), (3, 3), (4, 2)):
            for half, value in enumerate(spectrum(comp)):
                give(flat, odd * FIELDS + field, half, value)
            send(odd * FIELDS + field)
        t_xx, t_xy, t_yy = spectrum(0), spectrum(5), spectrum(1)
        for half in range(2):
            xi_y = waves_y(HALF, odd + 2 * half)
            give(flat, odd * FIELDS, half, xi_x * t_xx[half] + xi_y * t_xy[half])
            give(flat, odd * FIELDS + 1, half, xi_x * t_xy[half] + xi_y * t_yy[half])
        send(odd * FIELDS)
        send(odd * FIELDS + 1)
    for copy in copies:
        copy.wait()
    for index in range(N // TILE):
        keep(index).wait()


SHAPE = (LANE, BLOCKS, SUB, LANE)
SPACED = (LANE, BLOCKS + 1, SUB, LANE)
BUFFER = pltpu.HBM(SHAPE, f32)


def forward(order, conc, halos, kinetic, decay, unit, txf, mq):
    return pl.pallas_call(
        forward_body,
        in_specs=[RESIDENT] * 2 + [REMAIN] * 7,
        out_specs=(REMAIN, REMAIN),
        out_shape=(BUFFER, pltpu.HBM((N, N), f32)),
        scratch_shapes=[
            *[pltpu.VMEM((N, N), f32)] * 4,
            pltpu.VMEM((COMPS, N, N), f32),
            pltpu.VMEM(tables_of(2), bf16),
            pltpu.VMEM(tables_of(4), bf16),
            pltpu.VMEM((N, N), f32),
            pltpu.VMEM((COMPS, N, N), f32),
            pltpu.VMEM(SPACED, f32),
            pltpu.VMEM((2, COMPS * TILE, HALF), bf16),
            pltpu.VMEM((2, COMPS * TILE, HALF), bf16),
            pltpu.SemaphoreType.DMA((N // TILE, COMPS + 4)),
            pltpu.SemaphoreType.DMA((2,)),
            pltpu.SemaphoreType.DMA((N // TILE,)),
            pltpu.SemaphoreType.DMA((BLOCKS,)),
        ],
        compiler_params=params(40),
        name="forward",
    )(order, conc, *map(in_hbm, (*halos, kinetic, decay, unit, txf, mq)))


def middle_body(
    band_ref, in_ref, mz_hbm, out_ref, received, mz_ref, packed, in_sems, out_sems, table_sem
):
    source = received.reshape(LANE * PITCH, LANE)
    flat = packed.reshape(LANE * PITCH, LANE)

    def fetch(block):
        return pltpu.make_async_copy(in_ref.at[:, block], received.at[:, block], in_sems.at[block])

    def send(block):
        return pltpu.make_async_copy(packed.at[:, block], out_ref.at[:, block], out_sems.at[block])

    mz_copy = pltpu.make_async_copy(mz_hbm, mz_ref, table_sem)
    for field in range(FIELDS):
        fetch(field).start()
    mz_copy.start()
    for field in range(FIELDS):
        fetch(field).wait()
    for field in range(FIELDS):
        fetch(FIELDS + field).start()
    mz_copy.wait()

    def step(odd, carry):
        @pl.when(odd > 0)
        def _():
            for field in range(FIELDS):
                fetch(FIELDS + field).wait()

        middle_step(band_ref[0], source, mz_ref, flat, odd)
        for field in range(FIELDS):
            send(odd * FIELDS + field).start()
        return carry

    lax.fori_loop(0, 2, step, 0)
    for block in range(BLOCKS):
        send(block).wait()


def middle_step(band, source, mz_ref, flat, odd):
    onward = (mz_ref[0, 0], mz_ref[0, 1])
    backward = (mz_ref[1, 0], mz_ref[1, 1])
    fields = [
        [
            table_times(onward, take(source, odd * FIELDS + field, half))
            for field in range(FIELDS)
        ]
        for half in range(2)
    ]
    xi_x = waves_x(DEPTH)
    depth_index = lax.broadcasted_iota(jnp.int32, (DEPTH, HALF), 0)
    xi_z = jnp.where(depth_index < DEPTH // 2, depth_index, depth_index - DEPTH).astype(f32)
    for half in range(2):
        wave_y = band * RADIX + odd + 2 * half
        xi_y = jnp.where(wave_y < N // 2, wave_y, wave_y - N).astype(f32)
        wave_sq = xi_x * xi_x + xi_y * xi_y + xi_z * xi_z
        live = (wave_sq > 0.5) & (xi_x < float(HALF))
        safe = jnp.where(live, wave_sq, 1.0)
        inverse = 1.0 / safe
        first = jnp.where(live, (0.5 / shear_ref) * inverse, 0.0)
        second = jnp.where(live, (0.5 * coupling) * (inverse * inverse), 0.0)
        parts = []
        for rows in (slice(0, DEPTH), slice(DEPTH, 2 * DEPTH)):
            a_x, a_y, t_xz, t_yz, t_zz = (field[rows] for field in fields[half])
            v_x = a_x + t_xz * xi_z
            v_y = a_y + t_yz * xi_z
            v_z = t_xz * xi_x + t_yz * xi_y + t_zz * xi_z
            inner = (xi_x * v_x + xi_y * v_y + xi_z * v_z) * second
            h_x = v_x * first - xi_x * inner
            h_y = v_y * first - xi_y * inner
            h_z = v_z * first - xi_z * inner
            parts.append(
                (
                    h_x,
                    h_y,
                    xi_z * h_x + xi_x * h_z,
                    xi_z * h_y + xi_y * h_z,
                    2.0 * xi_z * h_z,
                )
            )
        for field in range(FIELDS):
            value = jnp.concatenate([parts[0][field], parts[1][field]], axis=0)
            give(flat, odd * FIELDS + field, half, table_times(backward, value))


def middle(band, received, mz):
    return pl.pallas_call(
        middle_body,
        in_specs=[SCALAR, REMAIN, REMAIN],
        out_specs=REMAIN,
        out_shape=BUFFER,
        scratch_shapes=[
            pltpu.VMEM(SPACED, f32),
            pltpu.VMEM(tables_of(2), bf16),
            pltpu.VMEM(SPACED, f32),
            pltpu.SemaphoreType.DMA((BLOCKS,)),
            pltpu.SemaphoreType.DMA((BLOCKS,)),
            pltpu.SemaphoreType.DMA(()),
        ],
        compiler_params=params(24),
        name="middle",
    )(band, in_hbm(received), in_hbm(mz))


def inverse_y(source, mqi_ref, comp):
    blocks = []
    for rest in range(RADIX):
        odd, half = rest % 2, rest // 2

        def field(index):
            return take(source, odd * FIELDS + index, half)

        if comp == 0:
            value = 2.0 * waves_x(HALF) * field(0)
        elif comp == 1:
            value = 2.0 * waves_y(HALF, rest) * field(1)
        elif comp == 5:
            value = waves_y(HALF, rest) * field(0) + waves_x(HALF) * field(1)
        else:
            value = field(6 - comp)
        result = table_times((mqi_ref[rest, 0], mqi_ref[rest, 1]), value)
        blocks.append((result[:LANE], result[LANE:]))
    er0, er1 = blocks[0][0] + blocks[2][0], blocks[0][0] - blocks[2][0]
    ei0, ei1 = blocks[0][1] + blocks[2][1], blocks[0][1] - blocks[2][1]
    or0, or1 = blocks[1][0] + blocks[3][0], blocks[1][0] - blocks[3][0]
    oi0, oi1 = blocks[1][1] + blocks[3][1], blocks[1][1] - blocks[3][1]
    return (
        (er0 + or0, ei0 + oi0),
        (er1 - oi1, ei1 + or1),
        (er0 - or0, ei0 - oi0),
        (er1 + oi1, ei1 - or1),
    )


def inverse_body(
    in_ref, strain_hbm, mqi_hbm, txi_hbm, out_ref, received, strain_ref, mqi_ref, txi_ref, moved,
    in_sems, strain_sems, table_sems, sems,
):
    source = received.reshape(LANE * PITCH, LANE)

    def fetch(field):
        return [
            pltpu.make_async_copy(in_ref.at[:, block], received.at[:, block], in_sems.at[block])
            for block in (field, FIELDS + field)
        ]

    def fetch_strain(comp):
        return [
            pltpu.make_async_copy(strain_hbm.at[comp], strain_ref.at[comp], strain_sems.at[comp])
        ]

    def copy_of(comp):
        return pltpu.make_async_copy(moved.at[comp], out_ref.at[comp], sems.at[comp])

    def start(copies):
        for copy in copies:
            copy.start()

    def wait(copies):
        for copy in copies:
            copy.wait()

    tables = [
        pltpu.make_async_copy(mqi_hbm, mqi_ref, table_sems.at[0]),
        pltpu.make_async_copy(txi_hbm, txi_ref, table_sems.at[1]),
    ]
    order = (4, 3, 2, 0, 1, 5)
    needs = ((2,), (3,), (4,), (0,), (1,), ())
    start(fetch(2))
    start(tables)
    wait(fetch(2))
    wait(tables)
    for comp, fields in zip(order, needs):
        start(fetch_strain(comp))
        for field in fields:
            if field != 2:
                start(fetch(field))

    planes = inverse_y(source, mqi_ref, order[0])
    for place, comp in enumerate(order):
        wait(fetch_strain(comp))
        if place + 1 < COMPS:
            for field in needs[place + 1]:
                wait(fetch(field))
            following = inverse_y(source, mqi_ref, order[place + 1])
        halves = []
        for parity in range(2):
            lanes = slice(LANE * parity, LANE * (parity + 1))
            value = jnp.concatenate(
                [jnp.concatenate([real[:, lanes], imag[:, lanes]], axis=1) for real, imag in planes],
                axis=0,
            )
            halves.append(times_table(value, (txi_ref[parity, 0], txi_ref[parity, 1])))
        even, odd = halves
        left = pl.ds(0, HALF)
        right = pl.ds(HALF, HALF)
        moved[comp, :, left] = strain_ref[comp, :, left] - (even + odd)
        moved[comp, :, right] = strain_ref[comp, :, right] - (even - odd)
        copy_of(comp).start()
        planes = following
    for comp in range(COMPS):
        copy_of(comp).wait()


def inverse(returned, strain, mqi, txi):
    return pl.pallas_call(
        inverse_body,
        in_specs=[REMAIN] * 4,
        out_specs=REMAIN,
        out_shape=pltpu.HBM((COMPS, N, N), f32),
        scratch_shapes=[
            pltpu.VMEM(SPACED, f32),
            pltpu.VMEM((COMPS, N, N), f32),
            pltpu.VMEM(tables_of(4), bf16),
            pltpu.VMEM(tables_of(2), bf16),
            pltpu.VMEM((COMPS, N, N), f32),
            pltpu.SemaphoreType.DMA((BLOCKS,)),
            pltpu.SemaphoreType.DMA((COMPS,)),
            pltpu.SemaphoreType.DMA((2,)),
            pltpu.SemaphoreType.DMA((COMPS,)),
        ],
        compiler_params=params(32),
        name="inverse",
    )(in_hbm(returned), in_hbm(strain), in_hbm(mqi), in_hbm(txi))


def exchange(block):
    packed = block.reshape(DEPTH, ROWS, LANE)
    moved = lax.all_to_all(packed, "gz", split_axis=0, concat_axis=0, tiled=True)
    return moved.reshape(SHAPE)


def neighbours(plane, count):
    ahead = [(i, (i + 1) % count) for i in range(count)]
    behind = [((i + 1) % count, i) for i in range(count)]
    return lax.ppermute(plane, "gz", ahead), lax.ppermute(plane, "gz", behind)


def shards(
    order_param,
    concentration,
    strain,
    grain_ids,
    seed_labels,
    grain_moduli,
    grain_mobility,
    seed_rate,
):
    count = lax.axis_size("gz")
    order_now = order_param.reshape(N, N)
    conc_now = concentration.reshape(N, N)
    planes = strain.reshape(COMPS, N, N)
    order_halos = neighbours(order_now, count)
    conc_halos = neighbours(conc_now, count)
    unit, kinetic, decay = coefficients(
        grain_moduli,
        grain_mobility,
        seed_rate,
        grain_ids.reshape(N, N),
        seed_labels.reshape(N, N),
        planes,
    )
    for _ in range(SUBSTEPS - 1):
        order_new = order_step(order_now, conc_now, order_halos, kinetic, decay)
        order_halos = neighbours(order_new, count)
        txf, mq = onward_tables(conc_halos[0])
        conc_new = conc_step(conc_now, order_now, order_new, conc_halos, (txf,))
        conc_halos = neighbours(conc_new, count)
        order_now, conc_now = order_new, conc_new
    spectra, order_next = forward(
        order_now, conc_now, order_halos, kinetic, decay, unit, txf, mq
    )
    band = lax.axis_index("gz").astype(jnp.int32).reshape(1)
    spectra, band, conc_halos = lax.optimization_barrier((spectra, band, conc_halos))
    received = exchange(spectra)
    mz, mqi, txi = backward_tables(band)
    conc_next = conc_step(conc_now, order_now, order_next, conc_halos)
    returned = exchange(middle(band, received, mz))
    strain_next = inverse(returned, planes, mqi, txi)
    return (
        order_next.reshape(1, N, N),
        conc_next.reshape(1, N, N),
        strain_next.reshape(COMPS, 1, N, N),
    )


def solution(mesh):
    return jax.shard_map(
        shards,
        mesh=mesh,
        in_specs=(
            P("gz", None, None),
            P("gz", None, None),
            P(None, "gz", None, None),
            P("gz", None, None),
            P("gz", None, None),
            P(),
            P(),
            P(),
        ),
        out_specs=(P("gz", None, None), P("gz", None, None), P(None, "gz", None, None)),
        check_vma=False,
    )
```

```python
import functools
import math

import jax
import jax.numpy as jnp
from jax import lax
from jax.experimental import pallas as pl
from jax.experimental.pallas import tpu as pltpu
from jax.sharding import PartitionSpec as P

SUBSTEPS = 2
N = 512
HALF = 256
LANE = 128
DEPTH = 128
COMPS = 6
RADIX = 4
FIELDS = 5
SUB = 8
BLOCKS = 2 * FIELDS
ROWS = BLOCKS * SUB
PITCH = (BLOCKS + 1) * SUB

time_step = 0.05
grad_coef = 1.0
well_height = 1.0
drive_coef = 2.0
conc_eq = 0.5
mech_boost = 1.0
diffusivity = 1.0
release_coef = 1.0
residual_stiff = 0.1
lame_ref = 1.0
shear_ref = 1.0
coupling = (lame_ref + shear_ref) / (shear_ref * (lame_ref + 2.0 * shear_ref))

f32 = jnp.float32
bf16 = jnp.bfloat16
MIB = 1024 * 1024


def params(mib, dims=0):
    semantics = ("arbitrary",) * dims if dims else None
    return pltpu.CompilerParams(dimension_semantics=semantics, vmem_limit_bytes=mib * MIB)


def in_hbm(value):
    return pltpu.with_memory_space_constraint(value, pltpu.HBM)


RESIDENT = pl.BlockSpec(memory_space=pltpu.VMEM)
REMAIN = pl.BlockSpec(memory_space=pl.ANY)
SCALAR = pl.BlockSpec(memory_space=pltpu.SMEM)


def split(value):
    high = value.astype(bf16)
    low = (value - high.astype(f32)).astype(bf16)
    return high, low


def mul(left, right):
    return lax.dot_general(
        left, right, (((1,), (0,)), ((), ())), preferred_element_type=f32
    )


def table_times(table, value):
    high, low = split(value)
    return mul(table[0], high) + mul(table[0], low) + mul(table[1], high)


def times_table(value, table):
    high, low = split(value)
    return mul(high, table[0]) + mul(low, table[0]) + mul(high, table[1])


def unit_cos(index):
    wrapped = ((index + 256) & 511) - 256
    angle = (128 - jnp.abs(wrapped)).astype(f32) * (2.0 * math.pi / 512.0)
    square = angle * angle
    poly = 1.0 / 6227020800.0
    for power in (39916800.0, 362880.0, 5040.0, 120.0, 6.0):
        poly = 1.0 / power - square * poly
    return angle * (1.0 - square * poly)


def table_grid():
    rows = lax.broadcasted_iota(jnp.int32, (HALF, HALF), 0)
    cols = lax.broadcasted_iota(jnp.int32, (HALF, HALF), 1)
    turn = ((rows >> 7) - (cols >> 7)) * 128
    return rows, cols, rows & 127, cols & 127, turn


def put(ref, slot, value):
    high, low = split(value)
    ref[slot, 0] = high
    ref[slot, 1] = low


def onward_body(order_ref, txf_ref, mq_ref):
    rows, cols, row_low, col_low, turn = table_grid()
    for parity in range(2):
        wave = 2 * col_low + parity
        put(txf_ref, parity, unit_cos(rows * wave + (cols >> 7) * 128))
    for rest in range(RADIX):
        put(mq_ref, rest, unit_cos((4 * row_low + rest) * col_low + turn))


def backward_body(order_ref, mz_ref, mqi_ref, txi_ref):
    rows, cols, row_low, col_low, turn = table_grid()
    for parity in range(2):
        wave = 2 * row_low + parity
        weight = jnp.where(wave == 0, 1.0, 2.0) * (1.0 / float(N * N * DEPTH))
        put(txi_ref, parity, unit_cos(wave * cols + (rows >> 7) * 128) * weight)
    for rest in range(RADIX):
        put(mqi_ref, rest, unit_cos((4 * col_low + rest) * row_low - turn))
    put(mz_ref, 0, unit_cos(4 * row_low * col_low + turn))
    put(mz_ref, 1, unit_cos(4 * row_low * col_low - turn))


def tables_of(count):
    return (count, 2, HALF, HALF)


def table_call(body, counts, name, operand, spec):
    return pl.pallas_call(
        body,
        in_specs=[spec],
        out_shape=tuple(pltpu.HBM(tables_of(count), bf16) for count in counts),
        out_specs=tuple(RESIDENT for _ in counts),
        compiler_params=params(8),
        name=name,
    )(operand)


def onward_tables(ready):
    return table_call(onward_body, (2, 4), "onward_tables", ready, REMAIN)


def backward_tables(ready):
    return table_call(backward_body, (2, 4, 2), "backward_tables", ready, SCALAR)


TILE = 128
STRIP = 16


def strips(rows, body):
    def step(index, carry):
        body(pl.multiple_of(index * STRIP, STRIP))
        return carry

    lax.fori_loop(0, rows // STRIP, step, 0, unroll=True)


def lane_table(read, count):
    lanes = lax.broadcasted_iota(jnp.int32, (STRIP, LANE), 1)
    table = jnp.zeros((STRIP, LANE), f32)
    for index in range(count):
        table = jnp.where(lanes == index, read(index), table)
    return table


def pick(table, index):
    parts = [
        jnp.take_along_axis(table, index[:, LANE * k : LANE * (k + 1)], axis=1)
        for k in range(N // LANE)
    ]
    return jnp.concatenate(parts, axis=1)


def rows_of(index):
    if isinstance(index, int):
        return pl.ds(index * TILE, TILE)
    return pl.ds(pl.multiple_of(index * TILE, TILE), TILE)


def stream(fetch, work, count=N // TILE):
    first = fetch(0)
    for copy in first:
        copy.start()
    for copy in first:
        copy.wait()
    for index in range(1, count):
        for copy in fetch(index):
            copy.start()

    def step(index, carry):
        @pl.when(index > 0)
        def _():
            for copy in fetch(index):
                copy.wait()

        work(index)
        return carry

    lax.fori_loop(0, count, step, 0)


def planes_of(source, target, rows, sems, index, base):
    return tuple(
        pltpu.make_async_copy(source.at[k, rows], target.at[k, rows], sems.at[index, base + k])
        for k in range(COMPS)
    )


def coef_body(
    moduli_hbm, mobility_hbm, rates_hbm, grain_ref, label_ref, strain_ref,
    unit_out, kin_out, dec_out, moduli, mobility, rates, lookup, sems,
):
    grains = mobility.shape[0]

    @pl.when(pl.program_id(0) == 0)
    def _():
        copies = [
            pltpu.make_async_copy(source, target, sems.at[k])
            for k, (source, target) in enumerate(
                ((moduli_hbm, moduli), (mobility_hbm, mobility), (rates_hbm, rates))
            )
        ]
        for copy in copies:
            copy.start()
        for copy in copies:
            copy.wait()
        lookup[0] = lane_table(lambda k: moduli[0, k], grains)
        lookup[1] = lane_table(lambda k: moduli[1, k], grains)
        lookup[2] = lane_table(lambda k: mobility[k], grains)
        lookup[3] = lane_table(lambda k: rates[k - 1] if k else 0.0, rates.shape[0] + 1)

    lames, shears, mobs, speeds = (lookup[k] for k in range(4))

    def strip(start):
        where = pl.ds(start, STRIP)
        grain = grain_ref[where, :]
        lame = pick(lames, grain)
        shear = pick(shears, grain)
        parts = [strain_ref[comp, where, :] for comp in range(COMPS)]
        trace = parts[0] + parts[1] + parts[2]
        square = (
            parts[0] * parts[0]
            + parts[1] * parts[1]
            + parts[2] * parts[2]
            + 2.0 * (parts[3] * parts[3] + parts[4] * parts[4] + parts[5] * parts[5])
        )
        energy = 0.5 * lame * trace * trace + shear * square
        mech = 1.0 + mech_boost * energy / (1.0 + energy)
        kin_out[where, :] = time_step * pick(mobs, grain) * mech
        dec_out[where, :] = time_step * pick(speeds, label_ref[where, :])
        spread = lame * trace
        double = 2.0 * shear
        for comp in range(COMPS):
            part = double * parts[comp]
            unit_out[comp, where, :] = part + spread if comp < 3 else part

    strips(TILE, strip)


PLANE = jax.ShapeDtypeStruct((N, N), f32)
TILES = N // TILE


def coefficients(moduli, mobility, rates, grain, label, strain):
    stripe = pl.BlockSpec((TILE, N), lambda i: (i, 0))
    stack = pl.BlockSpec((COMPS, TILE, N), lambda i: (0, i, 0))
    operands = (moduli, mobility, rates, grain, label, strain)
    return pl.pallas_call(
        coef_body,
        grid=(TILES,),
        in_specs=[REMAIN, REMAIN, REMAIN, stripe, stripe, stack],
        out_specs=[stack, stripe, stripe],
        out_shape=[pltpu.VMEM((COMPS, N, N), f32), pltpu.VMEM((N, N), f32), pltpu.VMEM((N, N), f32)],
        scratch_shapes=[
            pltpu.SMEM(moduli.shape, f32),
            pltpu.SMEM(mobility.shape, f32),
            pltpu.SMEM(rates.shape, f32),
            pltpu.VMEM((4, STRIP, LANE), f32),
            pltpu.SemaphoreType.DMA((3,)),
        ],
        compiler_params=params(16, 1),
        name="coefficients",
    )(*map(in_hbm, operands))


def planar_sum(ref, start):
    center = ref[pl.ds(start, STRIP), :]
    before_start = (start + N - 8) & (N - 1)
    after_start = (start + STRIP) & (N - 1)
    if not isinstance(start, int):
        before_start = pl.multiple_of(before_start, 8)
        after_start = pl.multiple_of(after_start, 8)
    before = ref[pl.ds(before_start, 8), :]
    after = ref[pl.ds(after_start, 8), :]
    tall = jnp.concatenate([before, center, after], axis=0)
    height = STRIP + 16
    above = pltpu.roll(tall, 1, 0)[8 : 8 + STRIP]
    below = pltpu.roll(tall, height - 1, 0)[8 : 8 + STRIP]
    sides = pltpu.roll(center, 1, 1) + pltpu.roll(center, N - 1, 1)
    return center, (above + below) + sides


def next_order(p_ref, start, halo_sum, conc_now, kinetic, decay):
    order_now, order_sum = planar_sum(p_ref, start)
    lap_order = order_sum + halo_sum - 6.0 * order_now
    slope = order_now * (1.0 - order_now)
    well_grad = 2.0 * slope * (1.0 - 2.0 * order_now)
    force = (
        grad_coef * lap_order
        - well_height * well_grad
        + drive_coef * 6.0 * slope * (conc_now - conc_eq)
    )
    return order_now + kinetic * force - decay * order_now


def tiles(body):
    def step(index, carry):
        base = pl.multiple_of(index * TILE, TILE)
        strips(TILE, lambda local: body(pl.multiple_of(base + local, STRIP)))
        return carry

    lax.fori_loop(0, N // TILE, step, 0)


def order_body(p_ref, c_ref, up_ref, down_ref, kin_ref, dec_ref, p_out):
    def strip(start):
        where = pl.ds(start, STRIP)
        p_out[where, :] = next_order(
            p_ref,
            start,
            up_ref[where, :] + down_ref[where, :],
            c_ref[where, :],
            kin_ref[where, :],
            dec_ref[where, :],
        )

    tiles(strip)


def order_step(order_now, conc_now, halos, kinetic, decay):
    planes = (order_now, conc_now, *halos, kinetic, decay)
    return pl.pallas_call(
        order_body,
        in_specs=[RESIDENT] * 6,
        out_specs=RESIDENT,
        out_shape=PLANE,
        compiler_params=params(8),
        name="order_step",
    )(*planes)


def next_conc(c_ref, start, halo_sum, order_now, order_new):
    conc_now, conc_sum = planar_sum(c_ref, start)
    lap_conc = conc_sum + halo_sum - 6.0 * conc_now
    return (
        conc_now + time_step * diffusivity * lap_conc + release_coef * (order_now - order_new)
    )


def conc_body(c_ref, p_ref, new_ref, up_ref, down_ref, *refs):
    c_out = refs[-1]

    def strip(start):
        where = pl.ds(start, STRIP)
        halo_sum = up_ref[where, :] + down_ref[where, :]
        c_out[where, :] = next_conc(c_ref, start, halo_sum, p_ref[where, :], new_ref[where, :])

    tiles(strip)


def conc_step(conc_now, order_now, order_new, halos, after=()):
    planes = (conc_now, order_now, order_new, *halos)
    return pl.pallas_call(
        conc_body,
        in_specs=[RESIDENT] * 5 + [REMAIN] * len(after),
        out_specs=RESIDENT,
        out_shape=PLANE,
        compiler_params=params(8),
        name="conc_step",
    )(*planes, *map(in_hbm, after))


def last_conc_body(c_ref, p_ref, new_ref, up_hbm, down_hbm, c_out, up_ref, down_ref, sems):
    halos = [
        pltpu.make_async_copy(up_hbm, up_ref, sems.at[0]),
        pltpu.make_async_copy(down_hbm, down_ref, sems.at[1]),
    ]
    for copy in halos:
        copy.start()
    for copy in halos:
        copy.wait()
    conc_body(c_ref, p_ref, new_ref, up_ref, down_ref, c_out)


def last_conc(conc_now, order_now, order_new, halos):
    return pl.pallas_call(
        last_conc_body,
        in_specs=[RESIDENT] * 3 + [REMAIN] * 2,
        out_specs=RESIDENT,
        out_shape=PLANE,
        scratch_shapes=[
            pltpu.VMEM((N, N), f32),
            pltpu.VMEM((N, N), f32),
            pltpu.SemaphoreType.DMA((2,)),
        ],
        compiler_params=params(8),
        name="last_conc",
    )(conc_now, order_now, order_new, *map(in_hbm, halos))


def waves_x(rows):
    lanes = lax.broadcasted_iota(jnp.int32, (rows, HALF), 1)
    return (2 * (lanes & (LANE - 1)) + (lanes >> 7)).astype(f32)


def waves_y(rows, rest):
    index = RADIX * (lax.broadcasted_iota(jnp.int32, (rows, HALF), 0) & (LANE - 1)) + rest
    return jnp.where(index < N // 2, index, index - N).astype(f32)


def give(flat, block, half, value):
    row = block * SUB + half * 4
    for parity in range(2):
        lanes = slice(LANE * parity, LANE * (parity + 1))
        flat[pl.ds(row + 2 * parity, LANE, stride=PITCH), :] = value[:LANE, lanes]
        flat[pl.ds(row + 2 * parity + 1, LANE, stride=PITCH), :] = value[LANE:, lanes]


def take(flat, block, half):
    row = block * SUB + half * 4
    parts = [
        jnp.concatenate(
            [flat[pl.ds(row + 2 * parity + k, LANE, stride=PITCH), :] for parity in range(2)],
            axis=1,
        )
        for k in range(2)
    ]
    return jnp.concatenate(parts, axis=0)


def both_parities(spectra, comp, j, shift):
    rows = pl.ds(LANE * j, LANE)
    return jnp.concatenate(
        [spectra[comp, rows, pl.ds(HALF * parity + shift, LANE)] for parity in range(2)], axis=1
    )


def butterflies(spectra, comp, odd):
    reals = [both_parities(spectra, comp, j, 0) for j in range(RADIX)]
    imags = [both_parities(spectra, comp, j, LANE) for j in range(RADIX)]
    if odd:
        er, ei = reals[0] - reals[2], imags[0] - imags[2]
        turned_r, turned_i = imags[1] - imags[3], reals[3] - reals[1]
    else:
        er, ei = reals[0] + reals[2], imags[0] + imags[2]
        turned_r, turned_i = reals[1] + reals[3], imags[1] + imags[3]
    return (
        jnp.concatenate([er + turned_r, ei + turned_i], axis=0),
        jnp.concatenate([er - turned_r, ei - turned_i], axis=0),
    )


def forward_body(
    p_ref, c_ref, up_hbm, down_hbm, kin_hbm, dec_hbm, unit_hbm, txf_hbm, mq_hbm,
    out_ref, p_hbm, up_ref, down_ref, kin_ref, dec_ref, unit_ref, txf_ref, mq_ref, p_out, spectra, packed,
    high_a, high_b, low_a, low_b,
    in_sems, table_sems, order_sems, sems,
):
    highs, lows = (high_a, high_b), (low_a, low_b)

    def fetch(index):
        rows = rows_of(index)
        singles = (
            (up_hbm, up_ref),
            (down_hbm, down_ref),
            (kin_hbm, kin_ref),
            (dec_hbm, dec_ref),
        )
        return (
            *(
                pltpu.make_async_copy(source.at[rows], target.at[rows], in_sems.at[index, COMPS + k])
                for k, (source, target) in enumerate(singles)
            ),
            *planes_of(unit_hbm, unit_ref, rows, in_sems, index, 0),
        )

    def keep(index):
        rows = rows_of(index)
        return pltpu.make_async_copy(p_out.at[rows], p_hbm.at[rows], order_sems.at[index])

    txf_copy = pltpu.make_async_copy(txf_hbm, txf_ref, table_sems.at[0])
    mq_copy = pltpu.make_async_copy(mq_hbm, mq_ref, table_sems.at[1])
    txf_copy.start()

    def stress_tile(index):
        slot = index % 2
        for local in range(0, TILE, STRIP):
            start = index * TILE + local
            where = pl.ds(start, STRIP)
            order = next_order(
                p_ref,
                start,
                up_ref[where, :] + down_ref[where, :],
                c_ref[where, :],
                kin_ref[where, :],
                dec_ref[where, :],
            )
            p_out[where, :] = order
            scale = order * order * (3.0 - 2.0 * order) + residual_stiff
            for comp in range(COMPS):
                part = scale * unit_ref[comp, where, :]
                left = part[:, :HALF]
                right = part[:, HALF:]
                here = pl.ds(comp * TILE + local, STRIP)
                for parity, folded in ((0, left + right), (1, left - right)):
                    highs[slot][parity, here, :], lows[slot][parity, here, :] = split(folded)
        keep(index).start()

    def transform_tile(index):
        slot = index % 2
        for parity in range(2):
            high = highs[slot][parity]
            result = (
                mul(high, txf_ref[parity, 0])
                + mul(lows[slot][parity], txf_ref[parity, 0])
                + mul(high, txf_ref[parity, 1])
            )
            for comp in range(COMPS):
                spectra[comp, pl.ds(index * TILE, TILE), pl.ds(HALF * parity, HALF)] = result[
                    comp * TILE : (comp + 1) * TILE
                ]

    for copy in fetch(0):
        copy.start()
    for copy in fetch(0):
        copy.wait()
    for index in range(1, TILES):
        for copy in fetch(index):
            copy.start()
    mq_copy.start()
    stress_tile(0)
    txf_copy.wait()
    for index in range(1, TILES):
        for copy in fetch(index):
            copy.wait()
        transform_tile(index - 1)
        stress_tile(index)
    transform_tile(TILES - 1)
    mq_copy.wait()

    flat = packed.reshape(LANE * PITCH, LANE)
    copies = []

    def send(block):
        copy = pltpu.make_async_copy(packed.at[:, block], out_ref.at[:, block], sems.at[block])
        copy.start()
        copies.append(copy)

    xi_x = waves_x(HALF)
    for odd in range(2):

        def spectrum(comp):
            return [
                table_times((mq_ref[odd + 2 * half, 0], mq_ref[odd + 2 * half, 1]), value)
                for half, value in enumerate(butterflies(spectra, comp, odd))
            ]

        for field, comp in ((2, 4), (3, 3), (4, 2)):
            for half, value in enumerate(spectrum(comp)):
                give(flat, odd * FIELDS + field, half, value)
            send(odd * FIELDS + field)
        t_xx, t_xy, t_yy = spectrum(0), spectrum(5), spectrum(1)
        for half in range(2):
            xi_y = waves_y(HALF, odd + 2 * half)
            give(flat, odd * FIELDS, half, xi_x * t_xx[half] + xi_y * t_xy[half])
            give(flat, odd * FIELDS + 1, half, xi_x * t_xy[half] + xi_y * t_yy[half])
        send(odd * FIELDS)
        send(odd * FIELDS + 1)
    for copy in copies:
        copy.wait()
    for index in range(N // TILE):
        keep(index).wait()


SHAPE = (LANE, BLOCKS, SUB, LANE)
SPACED = (LANE, BLOCKS + 1, SUB, LANE)
BUFFER = pltpu.HBM(SHAPE, f32)


def forward(order, conc, halos, kinetic, decay, unit, txf, mq):
    return pl.pallas_call(
        forward_body,
        in_specs=[RESIDENT] * 2 + [REMAIN] * 7,
        out_specs=(REMAIN, REMAIN),
        out_shape=(BUFFER, pltpu.HBM((N, N), f32)),
        scratch_shapes=[
            *[pltpu.VMEM((N, N), f32)] * 4,
            pltpu.VMEM((COMPS, N, N), f32),
            pltpu.VMEM(tables_of(2), bf16),
            pltpu.VMEM(tables_of(4), bf16),
            pltpu.VMEM((N, N), f32),
            pltpu.VMEM((COMPS, N, N), f32),
            pltpu.VMEM(SPACED, f32),
            *[pltpu.VMEM((2, COMPS * TILE, HALF), bf16)] * 4,
            pltpu.SemaphoreType.DMA((N // TILE, COMPS + 4)),
            pltpu.SemaphoreType.DMA((2,)),
            pltpu.SemaphoreType.DMA((N // TILE,)),
            pltpu.SemaphoreType.DMA((BLOCKS,)),
        ],
        compiler_params=params(44),
        name="forward",
    )(order, conc, *halos, *map(in_hbm, (kinetic, decay, unit, txf, mq)))


def middle_body(
    band_ref, in_ref, mz_hbm, out_ref, received, mz_ref, packed, in_sems, out_sems, table_sem
):
    source = received.reshape(LANE * PITCH, LANE)
    flat = packed.reshape(LANE * PITCH, LANE)

    def fetch(block):
        return pltpu.make_async_copy(in_ref.at[:, block], received.at[:, block], in_sems.at[block])

    def send(block):
        return pltpu.make_async_copy(packed.at[:, block], out_ref.at[:, block], out_sems.at[block])

    mz_copy = pltpu.make_async_copy(mz_hbm, mz_ref, table_sem)
    for field in range(FIELDS):
        fetch(field).start()
    mz_copy.start()
    for field in range(FIELDS):
        fetch(field).wait()
    for field in range(FIELDS):
        fetch(FIELDS + field).start()
    mz_copy.wait()

    def step(odd, carry):
        @pl.when(odd > 0)
        def _():
            for field in range(FIELDS):
                fetch(FIELDS + field).wait()

        middle_step(band_ref[0], source, mz_ref, flat, odd, lambda block: send(block).start())
        return carry

    lax.fori_loop(0, 2, step, 0)
    for block in range(BLOCKS):
        send(block).wait()


def middle_step(band, source, mz_ref, flat, odd, done):
    onward = (mz_ref[0, 0], mz_ref[0, 1])
    backward = (mz_ref[1, 0], mz_ref[1, 1])
    fields = [
        [
            table_times(onward, take(source, odd * FIELDS + field, half))
            for field in range(FIELDS)
        ]
        for half in range(2)
    ]
    xi_x = waves_x(DEPTH)
    depth_index = lax.broadcasted_iota(jnp.int32, (DEPTH, HALF), 0)
    xi_z = jnp.where(depth_index < DEPTH // 2, depth_index, depth_index - DEPTH).astype(f32)
    for half in range(2):
        wave_y = band * RADIX + odd + 2 * half
        xi_y = jnp.where(wave_y < N // 2, wave_y, wave_y - N).astype(f32)
        wave_sq = xi_x * xi_x + xi_y * xi_y + xi_z * xi_z
        live = (wave_sq > 0.5) & (xi_x < float(HALF))
        safe = jnp.where(live, wave_sq, 1.0)
        inverse = 1.0 / safe
        first = jnp.where(live, (0.5 / shear_ref) * inverse, 0.0)
        second = jnp.where(live, (0.5 * coupling) * (inverse * inverse), 0.0)
        parts = []
        for rows in (slice(0, DEPTH), slice(DEPTH, 2 * DEPTH)):
            a_x, a_y, t_xz, t_yz, t_zz = (field[rows] for field in fields[half])
            v_x = a_x + t_xz * xi_z
            v_y = a_y + t_yz * xi_z
            v_z = t_xz * xi_x + t_yz * xi_y + t_zz * xi_z
            inner = (xi_x * v_x + xi_y * v_y + xi_z * v_z) * second
            h_x = v_x * first - xi_x * inner
            h_y = v_y * first - xi_y * inner
            h_z = v_z * first - xi_z * inner
            parts.append(
                (
                    h_x,
                    h_y,
                    xi_z * h_x + xi_x * h_z,
                    xi_z * h_y + xi_y * h_z,
                    2.0 * xi_z * h_z,
                )
            )
        for field in range(FIELDS):
            value = jnp.concatenate([parts[0][field], parts[1][field]], axis=0)
            give(flat, odd * FIELDS + field, half, table_times(backward, value))
            if half == 1:
                done(odd * FIELDS + field)


def middle(band, received, mz):
    return pl.pallas_call(
        middle_body,
        in_specs=[SCALAR, REMAIN, REMAIN],
        out_specs=REMAIN,
        out_shape=BUFFER,
        scratch_shapes=[
            pltpu.VMEM(SPACED, f32),
            pltpu.VMEM(tables_of(2), bf16),
            pltpu.VMEM(SPACED, f32),
            pltpu.SemaphoreType.DMA((BLOCKS,)),
            pltpu.SemaphoreType.DMA((BLOCKS,)),
            pltpu.SemaphoreType.DMA(()),
        ],
        compiler_params=params(24),
        name="middle",
    )(band, in_hbm(received), in_hbm(mz))


def inverse_y(source, mqi_ref, comp):
    blocks = []
    for rest in range(RADIX):
        odd, half = rest % 2, rest // 2

        def field(index):
            return take(source, odd * FIELDS + index, half)

        if comp == 0:
            value = 2.0 * waves_x(HALF) * field(0)
        elif comp == 1:
            value = 2.0 * waves_y(HALF, rest) * field(1)
        elif comp == 5:
            value = waves_y(HALF, rest) * field(0) + waves_x(HALF) * field(1)
        else:
            value = field(6 - comp)
        result = table_times((mqi_ref[rest, 0], mqi_ref[rest, 1]), value)
        blocks.append((result[:LANE], result[LANE:]))
    er0, er1 = blocks[0][0] + blocks[2][0], blocks[0][0] - blocks[2][0]
    ei0, ei1 = blocks[0][1] + blocks[2][1], blocks[0][1] - blocks[2][1]
    or0, or1 = blocks[1][0] + blocks[3][0], blocks[1][0] - blocks[3][0]
    oi0, oi1 = blocks[1][1] + blocks[3][1], blocks[1][1] - blocks[3][1]
    return (
        (er0 + or0, ei0 + oi0),
        (er1 - oi1, ei1 + or1),
        (er0 - or0, ei0 - oi0),
        (er1 + oi1, ei1 - or1),
    )


def inverse_body(
    in_ref, strain_hbm, mqi_hbm, txi_hbm, out_ref, received, strain_ref, mqi_ref, txi_ref, moved,
    in_sems, strain_sems, table_sems, sems,
):
    source = received.reshape(LANE * PITCH, LANE)

    def fetch(field):
        return [
            pltpu.make_async_copy(in_ref.at[:, block], received.at[:, block], in_sems.at[block])
            for block in (field, FIELDS + field)
        ]

    def fetch_strain(comp):
        return [
            pltpu.make_async_copy(strain_hbm.at[comp], strain_ref.at[comp], strain_sems.at[comp])
        ]

    def copy_of(comp):
        return pltpu.make_async_copy(moved.at[comp], out_ref.at[comp], sems.at[comp])

    def start(copies):
        for copy in copies:
            copy.start()

    def wait(copies):
        for copy in copies:
            copy.wait()

    tables = [
        pltpu.make_async_copy(mqi_hbm, mqi_ref, table_sems.at[0]),
        pltpu.make_async_copy(txi_hbm, txi_ref, table_sems.at[1]),
    ]
    order = (4, 3, 2, 0, 1, 5)
    needs = ((2,), (3,), (4,), (0,), (1,), ())
    start(fetch(2))
    start(tables)
    wait(fetch(2))
    wait(tables)
    def start_for(place):
        if place < COMPS:
            for field in needs[place]:
                if field != 2:
                    start(fetch(field))
            start(fetch_strain(order[place]))

    for place in range(2):
        start_for(place)

    planes = inverse_y(source, mqi_ref, order[0])
    for place, comp in enumerate(order):
        start_for(place + 2)
        wait(fetch_strain(comp))
        if place + 1 < COMPS:
            for field in needs[place + 1]:
                wait(fetch(field))
            following = inverse_y(source, mqi_ref, order[place + 1])
        halves = []
        for parity in range(2):
            lanes = slice(LANE * parity, LANE * (parity + 1))
            value = jnp.concatenate(
                [jnp.concatenate([real[:, lanes], imag[:, lanes]], axis=1) for real, imag in planes],
                axis=0,
            )
            halves.append(times_table(value, (txi_ref[parity, 0], txi_ref[parity, 1])))
        even, odd = halves
        left = pl.ds(0, HALF)
        right = pl.ds(HALF, HALF)
        moved[comp, :, left] = strain_ref[comp, :, left] - (even + odd)
        moved[comp, :, right] = strain_ref[comp, :, right] - (even - odd)
        copy_of(comp).start()
        planes = following
    for comp in range(COMPS):
        copy_of(comp).wait()


def inverse(returned, strain, mqi, txi):
    return pl.pallas_call(
        inverse_body,
        in_specs=[REMAIN] * 4,
        out_specs=REMAIN,
        out_shape=pltpu.HBM((COMPS, N, N), f32),
        scratch_shapes=[
            pltpu.VMEM(SPACED, f32),
            pltpu.VMEM((COMPS, N, N), f32),
            pltpu.VMEM(tables_of(4), bf16),
            pltpu.VMEM(tables_of(2), bf16),
            pltpu.VMEM((COMPS, N, N), f32),
            pltpu.SemaphoreType.DMA((BLOCKS,)),
            pltpu.SemaphoreType.DMA((COMPS,)),
            pltpu.SemaphoreType.DMA((2,)),
            pltpu.SemaphoreType.DMA((COMPS,)),
        ],
        compiler_params=params(32),
        name="inverse",
    )(in_hbm(returned), in_hbm(strain), in_hbm(mqi), in_hbm(txi))


def exchange(block):
    packed = block.reshape(DEPTH, ROWS, LANE)
    moved = lax.all_to_all(packed, "gz", split_axis=0, concat_axis=0, tiled=True)
    return moved.reshape(SHAPE)


def neighbours(plane, count):
    ahead = [(i, (i + 1) % count) for i in range(count)]
    behind = [((i + 1) % count, i) for i in range(count)]
    return lax.ppermute(plane, "gz", ahead), lax.ppermute(plane, "gz", behind)


def shards(
    order_param,
    concentration,
    strain,
    grain_ids,
    seed_labels,
    grain_moduli,
    grain_mobility,
    seed_rate,
):
    count = lax.axis_size("gz")
    order_now = order_param.reshape(N, N)
    conc_now = concentration.reshape(N, N)
    planes = strain.reshape(COMPS, N, N)
    order_halos = neighbours(order_now, count)
    conc_halos = neighbours(conc_now, count)
    unit, kinetic, decay = coefficients(
        grain_moduli,
        grain_mobility,
        seed_rate,
        grain_ids.reshape(N, N),
        seed_labels.reshape(N, N),
        planes,
    )
    for _ in range(SUBSTEPS - 1):
        order_new = order_step(order_now, conc_now, order_halos, kinetic, decay)
        order_halos = neighbours(order_new, count)
        txf, mq = onward_tables(conc_halos[0])
        conc_new = conc_step(conc_now, order_now, order_new, conc_halos, (txf,))
        conc_halos = neighbours(conc_new, count)
        order_now, conc_now = order_new, conc_new
    spectra, order_next = forward(
        order_now, conc_now, order_halos, kinetic, decay, unit, txf, mq
    )
    band = lax.axis_index("gz").astype(jnp.int32).reshape(1)
    spectra, band, conc_halos = lax.optimization_barrier((spectra, band, conc_halos))
    received = exchange(spectra)
    mz, mqi, txi = backward_tables(band)
    conc_next = last_conc(conc_now, order_now, order_next, conc_halos)
    returned = exchange(middle(band, received, mz))
    strain_next = inverse(returned, planes, mqi, txi)
    return (
        order_next.reshape(1, N, N),
        conc_next.reshape(1, N, N),
        strain_next.reshape(COMPS, 1, N, N),
    )


def solution(mesh):
    return jax.shard_map(
        shards,
        mesh=mesh,
        in_specs=(
            P("gz", None, None),
            P("gz", None, None),
            P(None, "gz", None, None),
            P("gz", None, None),
            P("gz", None, None),
            P(),
            P(),
            P(),
        ),
        out_specs=(P("gz", None, None), P("gz", None, None), P(None, "gz", None, None)),
        check_vma=False,
    )
```

```python
import functools
import math

import jax
import jax.numpy as jnp
from jax import lax
from jax.experimental import pallas as pl
from jax.experimental.pallas import tpu as pltpu
from jax.sharding import PartitionSpec as P

SUBSTEPS = 2
N = 512
HALF = 256
LANE = 128
DEPTH = 128
COMPS = 6
RADIX = 4
FIELDS = 5
SUB = 8
BLOCKS = 2 * FIELDS
ROWS = BLOCKS * SUB
PITCH = (BLOCKS + 1) * SUB

time_step = 0.05
grad_coef = 1.0
well_height = 1.0
drive_coef = 2.0
conc_eq = 0.5
mech_boost = 1.0
diffusivity = 1.0
release_coef = 1.0
residual_stiff = 0.1
lame_ref = 1.0
shear_ref = 1.0
coupling = (lame_ref + shear_ref) / (shear_ref * (lame_ref + 2.0 * shear_ref))

f32 = jnp.float32
bf16 = jnp.bfloat16
MIB = 1024 * 1024


def params(mib, dims=0):
    semantics = ("arbitrary",) * dims if dims else None
    return pltpu.CompilerParams(dimension_semantics=semantics, vmem_limit_bytes=mib * MIB)


def in_hbm(value):
    return pltpu.with_memory_space_constraint(value, pltpu.HBM)


RESIDENT = pl.BlockSpec(memory_space=pltpu.VMEM)
REMAIN = pl.BlockSpec(memory_space=pl.ANY)
SCALAR = pl.BlockSpec(memory_space=pltpu.SMEM)


def split(value):
    high = value.astype(bf16)
    low = (value - high.astype(f32)).astype(bf16)
    return high, low


def mul(left, right):
    return lax.dot_general(
        left, right, (((1,), (0,)), ((), ())), preferred_element_type=f32
    )


def table_times(table, value):
    high, low = split(value)
    return mul(table[0], high) + mul(table[0], low) + mul(table[1], high)


def times_table(value, table):
    high, low = split(value)
    return mul(high, table[0]) + mul(low, table[0]) + mul(high, table[1])


def unit_cos(index):
    wrapped = ((index + 256) & 511) - 256
    angle = (128 - jnp.abs(wrapped)).astype(f32) * (2.0 * math.pi / 512.0)
    square = angle * angle
    poly = 1.0 / 6227020800.0
    for power in (39916800.0, 362880.0, 5040.0, 120.0, 6.0):
        poly = 1.0 / power - square * poly
    return angle * (1.0 - square * poly)


def table_grid():
    rows = lax.broadcasted_iota(jnp.int32, (HALF, HALF), 0)
    cols = lax.broadcasted_iota(jnp.int32, (HALF, HALF), 1)
    turn = ((rows >> 7) - (cols >> 7)) * 128
    return rows, cols, rows & 127, cols & 127, turn


def put(ref, slot, value):
    high, low = split(value)
    ref[slot, 0] = high
    ref[slot, 1] = low


def onward_body(order_ref, txf_ref, mq_ref):
    rows, cols, row_low, col_low, turn = table_grid()
    for parity in range(2):
        wave = 2 * col_low + parity
        put(txf_ref, parity, unit_cos(rows * wave + (cols >> 7) * 128))
    for rest in range(RADIX):
        put(mq_ref, rest, unit_cos((4 * row_low + rest) * col_low + turn))


def backward_body(order_ref, mz_ref, mqi_ref, txi_ref):
    rows, cols, row_low, col_low, turn = table_grid()
    for parity in range(2):
        wave = 2 * row_low + parity
        weight = jnp.where(wave == 0, 1.0, 2.0) * (1.0 / float(N * N * DEPTH))
        put(txi_ref, parity, unit_cos(wave * cols + (rows >> 7) * 128) * weight)
    for rest in range(RADIX):
        put(mqi_ref, rest, unit_cos((4 * col_low + rest) * row_low - turn))
    put(mz_ref, 0, unit_cos(4 * row_low * col_low + turn))
    put(mz_ref, 1, unit_cos(4 * row_low * col_low - turn))


def tables_of(count):
    return (count, 2, HALF, HALF)


def table_call(body, counts, name, operand, spec):
    return pl.pallas_call(
        body,
        in_specs=[spec],
        out_shape=tuple(pltpu.HBM(tables_of(count), bf16) for count in counts),
        out_specs=tuple(RESIDENT for _ in counts),
        compiler_params=params(8),
        name=name,
    )(operand)


def onward_tables(ready):
    return table_call(onward_body, (2, 4), "onward_tables", ready, REMAIN)


def backward_tables(ready):
    return table_call(backward_body, (2, 4, 2), "backward_tables", ready, SCALAR)


TILE = 128
STRIP = 16


def strips(rows, body):
    def step(index, carry):
        body(pl.multiple_of(index * STRIP, STRIP))
        return carry

    lax.fori_loop(0, rows // STRIP, step, 0, unroll=True)


def lane_table(read, count):
    lanes = lax.broadcasted_iota(jnp.int32, (STRIP, LANE), 1)
    table = jnp.zeros((STRIP, LANE), f32)
    for index in range(count):
        table = jnp.where(lanes == index, read(index), table)
    return table


def pick(table, index):
    parts = [
        jnp.take_along_axis(table, index[:, LANE * k : LANE * (k + 1)], axis=1)
        for k in range(N // LANE)
    ]
    return jnp.concatenate(parts, axis=1)


def rows_of(index):
    if isinstance(index, int):
        return pl.ds(index * TILE, TILE)
    return pl.ds(pl.multiple_of(index * TILE, TILE), TILE)


def stream(fetch, work, count=N // TILE):
    first = fetch(0)
    for copy in first:
        copy.start()
    for copy in first:
        copy.wait()
    for index in range(1, count):
        for copy in fetch(index):
            copy.start()

    def step(index, carry):
        @pl.when(index > 0)
        def _():
            for copy in fetch(index):
                copy.wait()

        work(index)
        return carry

    lax.fori_loop(0, count, step, 0)


def planes_of(source, target, rows, sems, index, base):
    return tuple(
        pltpu.make_async_copy(source.at[k, rows], target.at[k, rows], sems.at[index, base + k])
        for k in range(COMPS)
    )


def coef_body(
    moduli_hbm, mobility_hbm, rates_hbm, grain_ref, label_ref, strain_ref,
    unit_out, kin_out, dec_out, moduli, mobility, rates, lookup, sems,
):
    grains = mobility.shape[0]

    @pl.when(pl.program_id(0) == 0)
    def _():
        copies = [
            pltpu.make_async_copy(source, target, sems.at[k])
            for k, (source, target) in enumerate(
                ((moduli_hbm, moduli), (mobility_hbm, mobility), (rates_hbm, rates))
            )
        ]
        for copy in copies:
            copy.start()
        for copy in copies:
            copy.wait()
        lookup[0] = lane_table(lambda k: moduli[0, k], grains)
        lookup[1] = lane_table(lambda k: moduli[1, k], grains)
        lookup[2] = lane_table(lambda k: mobility[k], grains)
        lookup[3] = lane_table(lambda k: rates[k - 1] if k else 0.0, rates.shape[0] + 1)

    lames, shears, mobs, speeds = (lookup[k] for k in range(4))

    def strip(start):
        where = pl.ds(start, STRIP)
        grain = grain_ref[where, :]
        lame = pick(lames, grain)
        shear = pick(shears, grain)
        parts = [strain_ref[comp, where, :] for comp in range(COMPS)]
        trace = parts[0] + parts[1] + parts[2]
        square = (
            parts[0] * parts[0]
            + parts[1] * parts[1]
            + parts[2] * parts[2]
            + 2.0 * (parts[3] * parts[3] + parts[4] * parts[4] + parts[5] * parts[5])
        )
        energy = 0.5 * lame * trace * trace + shear * square
        mech = 1.0 + mech_boost * energy / (1.0 + energy)
        kin_out[where, :] = time_step * pick(mobs, grain) * mech
        dec_out[where, :] = time_step * pick(speeds, label_ref[where, :])
        spread = lame * trace
        double = 2.0 * shear
        for comp in range(COMPS):
            part = double * parts[comp]
            unit_out[comp, where, :] = part + spread if comp < 3 else part

    strips(TILE, strip)


PLANE = jax.ShapeDtypeStruct((N, N), f32)
TILES = N // TILE


def coefficients(moduli, mobility, rates, grain, label, strain):
    stripe = pl.BlockSpec((TILE, N), lambda i: (i, 0))
    stack = pl.BlockSpec((COMPS, TILE, N), lambda i: (0, i, 0))
    operands = (moduli, mobility, rates, grain, label, strain)
    return pl.pallas_call(
        coef_body,
        grid=(TILES,),
        in_specs=[REMAIN, REMAIN, REMAIN, stripe, stripe, stack],
        out_specs=[stack, stripe, stripe],
        out_shape=[pltpu.VMEM((COMPS, N, N), f32), pltpu.VMEM((N, N), f32), pltpu.VMEM((N, N), f32)],
        scratch_shapes=[
            pltpu.SMEM(moduli.shape, f32),
            pltpu.SMEM(mobility.shape, f32),
            pltpu.SMEM(rates.shape, f32),
            pltpu.VMEM((4, STRIP, LANE), f32),
            pltpu.SemaphoreType.DMA((3,)),
        ],
        compiler_params=params(16, 1),
        name="coefficients",
    )(*map(in_hbm, operands))


def planar_sum(ref, start):
    center = ref[pl.ds(start, STRIP), :]
    before_start = (start + N - 8) & (N - 1)
    after_start = (start + STRIP) & (N - 1)
    if not isinstance(start, int):
        before_start = pl.multiple_of(before_start, 8)
        after_start = pl.multiple_of(after_start, 8)
    before = ref[pl.ds(before_start, 8), :]
    after = ref[pl.ds(after_start, 8), :]
    tall = jnp.concatenate([before, center, after], axis=0)
    height = STRIP + 16
    above = pltpu.roll(tall, 1, 0)[8 : 8 + STRIP]
    below = pltpu.roll(tall, height - 1, 0)[8 : 8 + STRIP]
    sides = pltpu.roll(center, 1, 1) + pltpu.roll(center, N - 1, 1)
    return center, (above + below) + sides


def next_order(p_ref, start, halo_sum, conc_now, kinetic, decay):
    order_now, order_sum = planar_sum(p_ref, start)
    lap_order = order_sum + halo_sum - 6.0 * order_now
    slope = order_now * (1.0 - order_now)
    well_grad = 2.0 * slope * (1.0 - 2.0 * order_now)
    force = (
        grad_coef * lap_order
        - well_height * well_grad
        + drive_coef * 6.0 * slope * (conc_now - conc_eq)
    )
    return order_now + kinetic * force - decay * order_now


def tiles(body):
    def step(index, carry):
        base = pl.multiple_of(index * TILE, TILE)
        strips(TILE, lambda local: body(pl.multiple_of(base + local, STRIP)))
        return carry

    lax.fori_loop(0, N // TILE, step, 0)


def order_body(p_ref, c_ref, up_ref, down_ref, kin_ref, dec_ref, p_out):
    def strip(start):
        where = pl.ds(start, STRIP)
        p_out[where, :] = next_order(
            p_ref,
            start,
            up_ref[where, :] + down_ref[where, :],
            c_ref[where, :],
            kin_ref[where, :],
            dec_ref[where, :],
        )

    tiles(strip)


def order_step(order_now, conc_now, halos, kinetic, decay):
    planes = (order_now, conc_now, *halos, kinetic, decay)
    return pl.pallas_call(
        order_body,
        in_specs=[RESIDENT] * 6,
        out_specs=RESIDENT,
        out_shape=PLANE,
        compiler_params=params(8),
        name="order_step",
    )(*planes)


def next_conc(c_ref, start, halo_sum, order_now, order_new):
    conc_now, conc_sum = planar_sum(c_ref, start)
    lap_conc = conc_sum + halo_sum - 6.0 * conc_now
    return (
        conc_now + time_step * diffusivity * lap_conc + release_coef * (order_now - order_new)
    )


def conc_body(c_ref, p_ref, new_ref, up_ref, down_ref, *refs):
    c_out = refs[-1]

    def strip(start):
        where = pl.ds(start, STRIP)
        halo_sum = up_ref[where, :] + down_ref[where, :]
        c_out[where, :] = next_conc(c_ref, start, halo_sum, p_ref[where, :], new_ref[where, :])

    tiles(strip)


def conc_step(conc_now, order_now, order_new, halos, after=()):
    planes = (conc_now, order_now, order_new, *halos)
    return pl.pallas_call(
        conc_body,
        in_specs=[RESIDENT] * 5 + [REMAIN] * len(after),
        out_specs=RESIDENT,
        out_shape=PLANE,
        compiler_params=params(8),
        name="conc_step",
    )(*planes, *map(in_hbm, after))


def last_conc_body(c_ref, p_ref, new_ref, up_hbm, down_hbm, c_out, up_ref, down_ref, sems):
    halos = [
        pltpu.make_async_copy(up_hbm, up_ref, sems.at[0]),
        pltpu.make_async_copy(down_hbm, down_ref, sems.at[1]),
    ]
    for copy in halos:
        copy.start()
    for copy in halos:
        copy.wait()
    conc_body(c_ref, p_ref, new_ref, up_ref, down_ref, c_out)


def last_conc(conc_now, order_now, order_new, halos):
    return pl.pallas_call(
        last_conc_body,
        in_specs=[RESIDENT] * 3 + [REMAIN] * 2,
        out_specs=RESIDENT,
        out_shape=PLANE,
        scratch_shapes=[
            pltpu.VMEM((N, N), f32),
            pltpu.VMEM((N, N), f32),
            pltpu.SemaphoreType.DMA((2,)),
        ],
        compiler_params=params(8),
        name="last_conc",
    )(conc_now, order_now, order_new, *map(in_hbm, halos))


def waves_x(rows):
    lanes = lax.broadcasted_iota(jnp.int32, (rows, HALF), 1)
    return (2 * (lanes & (LANE - 1)) + (lanes >> 7)).astype(f32)


def waves_y(rows, rest):
    index = RADIX * (lax.broadcasted_iota(jnp.int32, (rows, HALF), 0) & (LANE - 1)) + rest
    return jnp.where(index < N // 2, index, index - N).astype(f32)


def give(flat, block, half, value):
    row = block * SUB + half * 4
    for parity in range(2):
        lanes = slice(LANE * parity, LANE * (parity + 1))
        flat[pl.ds(row + 2 * parity, LANE, stride=PITCH), :] = value[:LANE, lanes]
        flat[pl.ds(row + 2 * parity + 1, LANE, stride=PITCH), :] = value[LANE:, lanes]


def take(flat, block, half):
    row = block * SUB + half * 4
    parts = [
        jnp.concatenate(
            [flat[pl.ds(row + 2 * parity + k, LANE, stride=PITCH), :] for parity in range(2)],
            axis=1,
        )
        for k in range(2)
    ]
    return jnp.concatenate(parts, axis=0)


def both_parities(spectra, comp, j, shift):
    rows = pl.ds(LANE * j, LANE)
    return jnp.concatenate(
        [spectra[comp, rows, pl.ds(HALF * parity + shift, LANE)] for parity in range(2)], axis=1
    )


def butterflies(spectra, comp, odd):
    reals = [both_parities(spectra, comp, j, 0) for j in range(RADIX)]
    imags = [both_parities(spectra, comp, j, LANE) for j in range(RADIX)]
    if odd:
        er, ei = reals[0] - reals[2], imags[0] - imags[2]
        turned_r, turned_i = imags[1] - imags[3], reals[3] - reals[1]
    else:
        er, ei = reals[0] + reals[2], imags[0] + imags[2]
        turned_r, turned_i = reals[1] + reals[3], imags[1] + imags[3]
    return (
        jnp.concatenate([er + turned_r, ei + turned_i], axis=0),
        jnp.concatenate([er - turned_r, ei - turned_i], axis=0),
    )


def forward_body(
    p_ref, c_ref, up_hbm, down_hbm, kin_hbm, dec_hbm, unit_hbm, txf_hbm, mq_hbm,
    out_ref, p_hbm, up_ref, down_ref, kin_ref, dec_ref, unit_ref, txf_ref, mq_ref, p_out, spectra, packed,
    high_a, high_b, low_a, low_b,
    in_sems, table_sems, order_sems, sems,
):
    highs, lows = (high_a, high_b), (low_a, low_b)

    def fetch(index):
        rows = rows_of(index)
        singles = (
            (up_hbm, up_ref),
            (down_hbm, down_ref),
            (kin_hbm, kin_ref),
            (dec_hbm, dec_ref),
        )
        return (
            *(
                pltpu.make_async_copy(source.at[rows], target.at[rows], in_sems.at[index, COMPS + k])
                for k, (source, target) in enumerate(singles)
            ),
            *planes_of(unit_hbm, unit_ref, rows, in_sems, index, 0),
        )

    def keep(index):
        rows = rows_of(index)
        return pltpu.make_async_copy(p_out.at[rows], p_hbm.at[rows], order_sems.at[index])

    txf_copy = pltpu.make_async_copy(txf_hbm, txf_ref, table_sems.at[0])
    mq_copy = pltpu.make_async_copy(mq_hbm, mq_ref, table_sems.at[1])
    txf_copy.start()

    def stress_tile(index):
        slot = index % 2
        for local in range(0, TILE, STRIP):
            start = index * TILE + local
            where = pl.ds(start, STRIP)
            order = next_order(
                p_ref,
                start,
                up_ref[where, :] + down_ref[where, :],
                c_ref[where, :],
                kin_ref[where, :],
                dec_ref[where, :],
            )
            p_out[where, :] = order
            scale = order * order * (3.0 - 2.0 * order) + residual_stiff
            for comp in range(COMPS):
                part = scale * unit_ref[comp, where, :]
                left = part[:, :HALF]
                right = part[:, HALF:]
                here = pl.ds(comp * TILE + local, STRIP)
                for parity, folded in ((0, left + right), (1, left - right)):
                    highs[slot][parity, here, :], lows[slot][parity, here, :] = split(folded)
        keep(index).start()

    def transform_tile(index):
        slot = index % 2
        for parity in range(2):
            high = highs[slot][parity]
            result = (
                mul(high, txf_ref[parity, 0])
                + mul(lows[slot][parity], txf_ref[parity, 0])
                + mul(high, txf_ref[parity, 1])
            )
            for comp in range(COMPS):
                spectra[comp, pl.ds(index * TILE, TILE), pl.ds(HALF * parity, HALF)] = result[
                    comp * TILE : (comp + 1) * TILE
                ]

    for copy in fetch(0):
        copy.start()
    for copy in fetch(0):
        copy.wait()
    for index in range(1, TILES):
        for copy in fetch(index):
            copy.start()
    mq_copy.start()
    stress_tile(0)
    txf_copy.wait()
    for index in range(1, TILES):
        for copy in fetch(index):
            copy.wait()
        transform_tile(index - 1)
        stress_tile(index)
    transform_tile(TILES - 1)
    mq_copy.wait()

    flat = packed.reshape(LANE * PITCH, LANE)
    copies = []

    def send(block):
        copy = pltpu.make_async_copy(packed.at[:, block], out_ref.at[:, block], sems.at[block])
        copy.start()
        copies.append(copy)

    xi_x = waves_x(HALF)
    for odd in range(2):

        def spectrum(comp):
            return [
                table_times((mq_ref[odd + 2 * half, 0], mq_ref[odd + 2 * half, 1]), value)
                for half, value in enumerate(butterflies(spectra, comp, odd))
            ]

        for field, comp in ((2, 4), (3, 3), (4, 2)):
            for half, value in enumerate(spectrum(comp)):
                give(flat, odd * FIELDS + field, half, value)
            send(odd * FIELDS + field)
        t_xx, t_xy, t_yy = spectrum(0), spectrum(5), spectrum(1)
        for half in range(2):
            xi_y = waves_y(HALF, odd + 2 * half)
            give(flat, odd * FIELDS, half, xi_x * t_xx[half] + xi_y * t_xy[half])
            give(flat, odd * FIELDS + 1, half, xi_x * t_xy[half] + xi_y * t_yy[half])
        send(odd * FIELDS)
        send(odd * FIELDS + 1)
    for copy in copies:
        copy.wait()
    for index in range(N // TILE):
        keep(index).wait()


SHAPE = (LANE, BLOCKS, SUB, LANE)
SPACED = (LANE, BLOCKS + 1, SUB, LANE)
BUFFER = pltpu.HBM(SHAPE, f32)


def forward(order, conc, halos, kinetic, decay, unit, txf, mq):
    return pl.pallas_call(
        forward_body,
        in_specs=[RESIDENT] * 2 + [REMAIN] * 7,
        out_specs=(REMAIN, REMAIN),
        out_shape=(BUFFER, pltpu.HBM((N, N), f32)),
        scratch_shapes=[
            *[pltpu.VMEM((N, N), f32)] * 4,
            pltpu.VMEM((COMPS, N, N), f32),
            pltpu.VMEM(tables_of(2), bf16),
            pltpu.VMEM(tables_of(4), bf16),
            pltpu.VMEM((N, N), f32),
            pltpu.VMEM((COMPS, N, N), f32),
            pltpu.VMEM(SPACED, f32),
            *[pltpu.VMEM((2, COMPS * TILE, HALF), bf16)] * 4,
            pltpu.SemaphoreType.DMA((N // TILE, COMPS + 4)),
            pltpu.SemaphoreType.DMA((2,)),
            pltpu.SemaphoreType.DMA((N // TILE,)),
            pltpu.SemaphoreType.DMA((BLOCKS,)),
        ],
        compiler_params=params(44),
        name="forward",
    )(order, conc, *halos, *map(in_hbm, (kinetic, decay, unit, txf, mq)))


def middle_body(
    band_ref, in_ref, mz_hbm, out_ref, received, mz_ref, packed, in_sems, out_sems, table_sem
):
    source = received.reshape(LANE * PITCH, LANE)
    flat = packed.reshape(LANE * PITCH, LANE)

    def fetch(block):
        return pltpu.make_async_copy(in_ref.at[:, block], received.at[:, block], in_sems.at[block])

    def send(block):
        return pltpu.make_async_copy(packed.at[:, block], out_ref.at[:, block], out_sems.at[block])

    mz_copy = pltpu.make_async_copy(mz_hbm, mz_ref, table_sem)
    for field in range(FIELDS):
        fetch(field).start()
    mz_copy.start()
    for field in range(FIELDS):
        fetch(field).wait()
    for field in range(FIELDS):
        fetch(FIELDS + field).start()
    mz_copy.wait()

    def step(odd, carry):
        @pl.when(odd > 0)
        def _():
            for field in range(FIELDS):
                fetch(FIELDS + field).wait()

        middle_step(band_ref[0], source, mz_ref, flat, odd, lambda block: send(block).start())
        return carry

    lax.fori_loop(0, 2, step, 0)
    for block in range(BLOCKS):
        send(block).wait()


def middle_step(band, source, mz_ref, flat, odd, done):
    onward = (mz_ref[0, 0], mz_ref[0, 1])
    backward = (mz_ref[1, 0], mz_ref[1, 1])
    fields = [
        [
            table_times(onward, take(source, odd * FIELDS + field, half))
            for field in range(FIELDS)
        ]
        for half in range(2)
    ]
    xi_x = waves_x(DEPTH)
    depth_index = lax.broadcasted_iota(jnp.int32, (DEPTH, HALF), 0)
    xi_z = jnp.where(depth_index < DEPTH // 2, depth_index, depth_index - DEPTH).astype(f32)
    for half in range(2):
        wave_y = band * RADIX + odd + 2 * half
        xi_y = jnp.where(wave_y < N // 2, wave_y, wave_y - N).astype(f32)
        wave_sq = xi_x * xi_x + xi_y * xi_y + xi_z * xi_z
        live = (wave_sq > 0.5) & (xi_x < float(HALF))
        safe = jnp.where(live, wave_sq, 1.0)
        inverse = 1.0 / safe
        first = jnp.where(live, (0.5 / shear_ref) * inverse, 0.0)
        second = jnp.where(live, (0.5 * coupling) * (inverse * inverse), 0.0)
        parts = []
        for rows in (slice(0, DEPTH), slice(DEPTH, 2 * DEPTH)):
            a_x, a_y, t_xz, t_yz, t_zz = (field[rows] for field in fields[half])
            v_x = a_x + t_xz * xi_z
            v_y = a_y + t_yz * xi_z
            v_z = t_xz * xi_x + t_yz * xi_y + t_zz * xi_z
            inner = (xi_x * v_x + xi_y * v_y + xi_z * v_z) * second
            h_x = v_x * first - xi_x * inner
            h_y = v_y * first - xi_y * inner
            h_z = v_z * first - xi_z * inner
            parts.append(
                (
                    h_x,
                    h_y,
                    xi_z * h_x + xi_x * h_z,
                    xi_z * h_y + xi_y * h_z,
                    2.0 * xi_z * h_z,
                )
            )
        for field in range(FIELDS):
            value = jnp.concatenate([parts[0][field], parts[1][field]], axis=0)
            give(flat, odd * FIELDS + field, half, table_times(backward, value))
            if half == 1:
                done(odd * FIELDS + field)


def middle(band, received, mz):
    return pl.pallas_call(
        middle_body,
        in_specs=[SCALAR, REMAIN, REMAIN],
        out_specs=REMAIN,
        out_shape=BUFFER,
        scratch_shapes=[
            pltpu.VMEM(SPACED, f32),
            pltpu.VMEM(tables_of(2), bf16),
            pltpu.VMEM(SPACED, f32),
            pltpu.SemaphoreType.DMA((BLOCKS,)),
            pltpu.SemaphoreType.DMA((BLOCKS,)),
            pltpu.SemaphoreType.DMA(()),
        ],
        compiler_params=params(24),
        name="middle",
    )(band, in_hbm(received), in_hbm(mz))


def inverse_y(source, mqi_ref, comp):
    blocks = []
    for rest in range(RADIX):
        odd, half = rest % 2, rest // 2

        def field(index):
            return take(source, odd * FIELDS + index, half)

        if comp == 0:
            value = 2.0 * waves_x(HALF) * field(0)
        elif comp == 1:
            value = 2.0 * waves_y(HALF, rest) * field(1)
        elif comp == 5:
            value = waves_y(HALF, rest) * field(0) + waves_x(HALF) * field(1)
        else:
            value = field(6 - comp)
        result = table_times((mqi_ref[rest, 0], mqi_ref[rest, 1]), value)
        blocks.append((result[:LANE], result[LANE:]))
    er0, er1 = blocks[0][0] + blocks[2][0], blocks[0][0] - blocks[2][0]
    ei0, ei1 = blocks[0][1] + blocks[2][1], blocks[0][1] - blocks[2][1]
    or0, or1 = blocks[1][0] + blocks[3][0], blocks[1][0] - blocks[3][0]
    oi0, oi1 = blocks[1][1] + blocks[3][1], blocks[1][1] - blocks[3][1]
    return (
        (er0 + or0, ei0 + oi0),
        (er1 - oi1, ei1 + or1),
        (er0 - or0, ei0 - oi0),
        (er1 + oi1, ei1 - or1),
    )


def inverse_body(
    in_ref, strain_hbm, mqi_hbm, txi_hbm, out_ref, received, strain_ref, mqi_ref, txi_ref, moved,
    in_sems, strain_sems, table_sems, sems,
):
    source = received.reshape(LANE * PITCH, LANE)

    def fetch(field):
        return [
            pltpu.make_async_copy(in_ref.at[:, block], received.at[:, block], in_sems.at[block])
            for block in (field, FIELDS + field)
        ]

    def fetch_strain(comp):
        return [
            pltpu.make_async_copy(strain_hbm.at[comp], strain_ref.at[comp], strain_sems.at[comp])
        ]

    def copy_of(comp):
        return pltpu.make_async_copy(moved.at[comp], out_ref.at[comp], sems.at[comp])

    def start(copies):
        for copy in copies:
            copy.start()

    def wait(copies):
        for copy in copies:
            copy.wait()

    tables = [
        pltpu.make_async_copy(mqi_hbm, mqi_ref, table_sems.at[0]),
        pltpu.make_async_copy(txi_hbm, txi_ref, table_sems.at[1]),
    ]
    order = (4, 3, 2, 0, 1, 5)
    needs = ((2,), (3,), (4,), (0,), (1,), ())
    start(fetch(2))
    start(tables)
    wait(fetch(2))
    wait(tables)
    def start_for(place):
        if place < COMPS:
            for field in needs[place]:
                if field != 2:
                    start(fetch(field))
            start(fetch_strain(order[place]))

    for place in range(2):
        start_for(place)

    planes = inverse_y(source, mqi_ref, order[0])
    for place, comp in enumerate(order):
        start_for(place + 2)
        wait(fetch_strain(comp))
        if place + 1 < COMPS:
            for field in needs[place + 1]:
                wait(fetch(field))
            following = inverse_y(source, mqi_ref, order[place + 1])
        halves = []
        for parity in range(2):
            lanes = slice(LANE * parity, LANE * (parity + 1))
            value = jnp.concatenate(
                [jnp.concatenate([real[:, lanes], imag[:, lanes]], axis=1) for real, imag in planes],
                axis=0,
            )
            halves.append(times_table(value, (txi_ref[parity, 0], txi_ref[parity, 1])))
        even, odd = halves
        left = pl.ds(0, HALF)
        right = pl.ds(HALF, HALF)
        moved[comp, :, left] = strain_ref[comp, :, left] - (even + odd)
        moved[comp, :, right] = strain_ref[comp, :, right] - (even - odd)
        copy_of(comp).start()
        planes = following
    for comp in range(COMPS):
        copy_of(comp).wait()


def inverse(returned, strain, mqi, txi):
    return pl.pallas_call(
        inverse_body,
        in_specs=[REMAIN] * 4,
        out_specs=REMAIN,
        out_shape=pltpu.HBM((COMPS, N, N), f32),
        scratch_shapes=[
            pltpu.VMEM(SPACED, f32),
            pltpu.VMEM((COMPS, N, N), f32),
            pltpu.VMEM(tables_of(4), bf16),
            pltpu.VMEM(tables_of(2), bf16),
            pltpu.VMEM((COMPS, N, N), f32),
            pltpu.SemaphoreType.DMA((BLOCKS,)),
            pltpu.SemaphoreType.DMA((COMPS,)),
            pltpu.SemaphoreType.DMA((2,)),
            pltpu.SemaphoreType.DMA((COMPS,)),
        ],
        compiler_params=params(32),
        name="inverse",
    )(in_hbm(returned), in_hbm(strain), in_hbm(mqi), in_hbm(txi))


def exchange(block):
    packed = block.reshape(DEPTH, ROWS, LANE)
    moved = lax.all_to_all(packed, "gz", split_axis=0, concat_axis=0, tiled=True)
    return moved.reshape(SHAPE)


def neighbours(plane, count):
    ahead = [(i, (i + 1) % count) for i in range(count)]
    behind = [((i + 1) % count, i) for i in range(count)]
    return lax.ppermute(plane, "gz", ahead), lax.ppermute(plane, "gz", behind)


def shards(
    order_param,
    concentration,
    strain,
    grain_ids,
    seed_labels,
    grain_moduli,
    grain_mobility,
    seed_rate,
):
    count = lax.axis_size("gz")
    order_now = order_param.reshape(N, N)
    conc_now = concentration.reshape(N, N)
    planes = strain.reshape(COMPS, N, N)
    order_halos = neighbours(order_now, count)
    conc_halos = neighbours(conc_now, count)
    unit, kinetic, decay = coefficients(
        grain_moduli,
        grain_mobility,
        seed_rate,
        grain_ids.reshape(N, N),
        seed_labels.reshape(N, N),
        planes,
    )
    for _ in range(SUBSTEPS - 1):
        order_new = order_step(order_now, conc_now, order_halos, kinetic, decay)
        order_halos = neighbours(order_new, count)
        txf, mq = onward_tables(conc_halos[0])
        conc_new = conc_step(conc_now, order_now, order_new, conc_halos, (txf,))
        conc_halos = neighbours(conc_new, count)
        order_now, conc_now = order_new, conc_new
    spectra, order_next = forward(
        order_now, conc_now, order_halos, kinetic, decay, unit, txf, mq
    )
    band = lax.axis_index("gz").astype(jnp.int32).reshape(1)
    order_next, ready, conc_halos = lax.optimization_barrier((order_next, band, conc_halos))
    received = exchange(spectra)
    mz, mqi, txi = backward_tables(ready)
    conc_next = last_conc(conc_now, order_now, order_next, conc_halos)
    returned = exchange(middle(band, received, mz))
    strain_next = inverse(returned, planes, mqi, txi)
    return (
        order_next.reshape(1, N, N),
        conc_next.reshape(1, N, N),
        strain_next.reshape(COMPS, 1, N, N),
    )


def solution(mesh):
    return jax.shard_map(
        shards,
        mesh=mesh,
        in_specs=(
            P("gz", None, None),
            P("gz", None, None),
            P(None, "gz", None, None),
            P("gz", None, None),
            P("gz", None, None),
            P(),
            P(),
            P(),
        ),
        out_specs=(P("gz", None, None), P("gz", None, None), P(None, "gz", None, None)),
        check_vma=False,
    )
```
